256 devices in a mesh: grp: 32 (over y, x, core), hd: 8 (over z).
Axes of the slice: x: 4, y: 4, z: 8, core: 2. Of those that a mesh axis runs over, the one named last changes fastest.
Arguments:
- queries: bfloat16 [65536, 1024], P(('grp', 'hd')), may hold values from -8 to 8
- keys: bfloat16 [65536, 1024], P(('grp', 'hd')), may hold values from -8 to 8
- values: bfloat16 [65536, 1024], P(('grp', 'hd')), may hold values from -6 to 6
- grad_out: bfloat16 [65536, 1024], P(('grp', 'hd')), may hold values from -6 to 6
- neighbours: int32 [256, 8], replicated, may hold values from 0 to 255, as said below
Outputs:
- attended: bfloat16 [65536, 1024], P(('grp', 'hd'))
- grad_queries: bfloat16 [65536, 1024], P(('grp', 'hd'))
- grad_keys: bfloat16 [65536, 1024], P(('grp', 'hd'))
- grad_values: bfloat16 [65536, 1024], P(('grp', 'hd'))
The draws below stay inside these ranges and needn't reach their ends.
Inputs may be any that keep to these rules, and one draw needn't show every extreme that they name: `neighbours`: each block lists 8 distinct blocks, none of its own group (blocks g * 8 to g * 8 + 7 form group g). The blocks of one group list at most one block of any other group, and each block that a group lists is listed by exactly 4 of its blocks.
All inputs are finite; a program needn't handle non-finite values.
Results may differ from the reference program's by a relative error of at most 0.008.
Values may be sent and summed in bfloat16 or wider, within the bound.
A program may use at most 128 MiB of HBM per device.

```python
import jax
import jax.numpy as jnp
from jax import lax

HEADS = 8
HEAD_DIM = 128
D = 1024
BLK = 256
BLK_GRP = 8
NB = 8
NPART = 16
NBLK = 256
AGENTS = 65536


def drawn_pair(key):
    base_query = jax.random.fold_in(key, 11)
    base_key = jax.random.fold_in(key, 12)
    queries = jnp.clip(jax.random.normal(base_query, (AGENTS, D), jnp.float32), -6.0, 6.0)
    keys = jnp.clip(jax.random.normal(base_key, (AGENTS, D), jnp.float32), -6.0, 6.0)
    return (queries, keys)


def draw_queries(key, part):
    return drawn_pair(key)[0].astype(jnp.bfloat16)


def draw_keys(key, part):
    return drawn_pair(key)[1].astype(jnp.bfloat16)


def draw_neighbours(key, part):
    groups = NBLK // BLK_GRP

    def one_group(index):
        sub_key = jax.random.fold_in(key, index)
        order = jax.random.permutation(jax.random.fold_in(sub_key, 1), groups - 1)[:NPART].astype(jnp.int32)
        partners = order + (order >= index).astype(jnp.int32)
        within = jax.random.randint(jax.random.fold_in(sub_key, 2), (NPART,), 0, BLK_GRP).astype(jnp.int32)
        chosen = partners * BLK_GRP + within
        positions = jnp.arange(BLK_GRP, dtype=jnp.int32)[:, None] * (NB // 2) + jnp.arange(NB, dtype=jnp.int32)[None, :]
        return chosen[positions % NPART]
    listed = jax.vmap(one_group)(jnp.arange(groups, dtype=jnp.int32))
    return listed.reshape(NBLK, NB).astype(jnp.int32)


def block_levels(rng, shape, pieces, smallest, largest):
    def one(dim, parts):
        heights = jax.random.uniform(jax.random.fold_in(jax.random.fold_in(rng, 6), dim), (parts,), jnp.float32, smallest / len(pieces), largest / len(pieces))
        return jnp.repeat(jnp.exp(heights), shape[dim] // parts).reshape((-1,) + (1,) * (len(shape) - dim - 1))

    gain = one(*pieces[0])
    for cut in pieces[1:]:
        gain = gain * one(*cut)
    return gain


def scatter_about(stream_key, dims, width, most, pieces=(), held_as=jnp.bfloat16):
    loudness = block_levels(stream_key, dims, pieces, -0.22, 0.18) if pieces else 1.0
    values = jax.random.normal(stream_key, dims, jnp.float32) * width * loudness
    return jnp.minimum(jnp.maximum(values, -most), most).astype(held_as)


def setup_inputs(seed: int = 0) -> dict:
    streams_of = jax.random.split(jax.random.key(seed), 6)
    queries = draw_queries(jax.random.fold_in(streams_of[5], 71), 0)
    keys = draw_keys(jax.random.fold_in(streams_of[5], 71), 0)
    values = scatter_about(streams_of[2], (AGENTS, D), 1.0, 6.0, ((0, 256),))
    grad_out = scatter_about(streams_of[3], (AGENTS, D), 1.0, 6.0, ((0, 256),))
    neighbours = draw_neighbours(jax.random.fold_in(streams_of[5], 71), 0)
    return {"queries": queries, "keys": keys, "values": values, "grad_out": grad_out, "neighbours": neighbours}


def block_pass(query_blk, key_set, value_set, grad_blk, score_scale):
    query_full = query_blk.astype(jnp.float32)
    key_full = key_set.astype(jnp.float32)
    value_full = value_set.astype(jnp.float32)
    grad_full = grad_blk.astype(jnp.float32)
    scores = jnp.einsum("qhd,khd->hqk", query_full, key_full) * score_scale
    row_max = jnp.max(scores, axis=2, keepdims=True)
    exp_scores = jnp.exp(scores - row_max)
    weights = exp_scores / jnp.sum(exp_scores, axis=2, keepdims=True)
    weights_half = lax.optimization_barrier(weights.astype(jnp.bfloat16)).astype(jnp.float32)
    attended_full = jnp.einsum("hqk,khd->qhd", weights_half, value_full)
    row_delta = jnp.sum(grad_full * attended_full, axis=2)
    grad_weights = jnp.einsum("qhd,khd->hqk", grad_full, value_full)
    grad_scores = weights * (grad_weights - jnp.transpose(row_delta)[:, :, None])
    grad_scores = lax.optimization_barrier(grad_scores.astype(jnp.bfloat16)).astype(jnp.float32)
    grad_query = jnp.einsum("hqk,khd->qhd", grad_scores, key_full) * score_scale
    grad_key = jnp.einsum("hqk,qhd->khd", grad_scores, query_full) * score_scale
    grad_value = jnp.einsum("hqk,qhd->khd", weights_half, grad_full)
    return attended_full, grad_query, grad_key, grad_value


def reference(queries, keys, values, grad_out, neighbours):
    block_count = neighbours.shape[0]
    listed_count = neighbours.shape[1]
    tiles = (block_count, BLK, HEADS, HEAD_DIM)
    query_tiles = queries.reshape(tiles)
    key_tiles = keys.reshape(tiles)
    value_tiles = values.reshape(tiles)
    grad_tiles = grad_out.reshape(tiles)
    score_scale = HEAD_DIM ** -0.5

    def visit(carry, block):
        key_acc, value_acc = carry
        members = jnp.concatenate([block[None], neighbours[block]]).astype(jnp.int32)
        key_set = jnp.take(key_tiles, members, axis=0).reshape(-1, HEADS, HEAD_DIM)
        value_set = jnp.take(value_tiles, members, axis=0).reshape(-1, HEADS, HEAD_DIM)
        attended_full, grad_query, grad_key, grad_value = block_pass(
            query_tiles[block], key_set, value_set, grad_tiles[block], score_scale)
        key_acc = key_acc.at[members].add(grad_key.reshape(listed_count + 1, BLK, HEADS, HEAD_DIM))
        value_acc = value_acc.at[members].add(grad_value.reshape(listed_count + 1, BLK, HEADS, HEAD_DIM))
        return (key_acc, value_acc), (attended_full.astype(jnp.bfloat16), grad_query.astype(jnp.bfloat16))

    zeros = jnp.zeros(tiles, jnp.float32)
    (key_acc, value_acc), (attended, grad_queries) = lax.scan(
        visit, (zeros, zeros), jnp.arange(block_count, dtype=jnp.int32))
    full_shape = queries.shape
    return (attended.reshape(full_shape), grad_queries.reshape(full_shape),
            key_acc.astype(jnp.bfloat16).reshape(full_shape), value_acc.astype(jnp.bfloat16).reshape(full_shape))
```

```python
import jax
import jax.numpy as jnp
from jax import lax
from jax.experimental import pallas as pl
from jax.experimental.pallas import tpu as pltpu
from jax.sharding import PartitionSpec as P

MESH = pl.DeviceIdType.MESH
HD = 8
GRP = 32
ROWS = 256
W = 128
F32 = jnp.float32
BF16 = jnp.bfloat16
SCALE = W ** (-0.5)

PLACES = [(0, 1), (1, 0), (0, 3), (3, 0), (0, 2), (2, 0), (1, 1), (3, 3), (1, 3), (3, 1), (2, 2), (1, 2), (2, 1), (3, 2), (2, 3), (0, 0)]
XY_ORDER = [dy * 8 + dx * 2 + dc for dc in (0, 1) for dy, dx in PLACES if dy + dx + dc > 0]
Z_ORDER = [1, 7, 2, 6, 3, 5, 4]


def opposite(r):
    return ((4 - r // 8) % 4) * 8 + ((4 - (r // 2) % 4) % 4) * 2 + r % 2


def xy_group(g, r):
    c, x, y = g % 2, (g // 2) % 4, g // 8
    return (((y + r // 8) % 4) * 4 + (x + (r // 2) % 4) % 4) * 2 + (c + r % 2) % 2


def greet(g, z):
    barrier = pltpu.get_barrier_semaphore()
    for r in XY_ORDER:
        pl.semaphore_signal(barrier, inc=1, device_id={"grp": xy_group(g, r), "hd": z}, device_id_type=MESH)
    for d in Z_ORDER:
        pl.semaphore_signal(barrier, inc=1, device_id={"grp": g, "hd": (z + d) % HD}, device_id_type=MESH)
    pl.semaphore_wait(barrier, len(XY_ORDER) + len(Z_ORDER))


HALF = ROWS // 2
IN_PARTS = [("k", 0, HALF), ("k", HALF, HALF), ("v", 0, ROWS)]
OUT_PARTS = [("k", 0, ROWS), ("v", 0, HALF), ("v", HALF, HALF)]


def gather_kernel(picked, q, k, v, do, qh, kh, vh, doh, kgot, vgot, *scr):
    np_ = len(IN_PARTS)
    bufs, sends = scr[:np_], scr[np_ : 2 * np_]
    zs, zr, xs, xr, ls = scr[2 * np_ :]
    g, z = lax.axis_index("grp"), lax.axis_index("hd")
    greet(g, z)
    src = {"k": k, "v": v}
    own_out = {"k": kh, "v": vh}
    got = {"k": kgot, "v": vgot}
    mine = pl.ds(pl.multiple_of(z * W, W), W)

    jobs = [(src[a], r0, n, bufs[i].at[z]) for i, (a, r0, n) in enumerate(IN_PARTS)]
    jobs += [(q, 0, ROWS, qh.at[z]), (do, 0, ROWS, doh.at[z])]

    def z_copy(j, i, d):
        s, r0, n, dst = jobs[j]
        t = (z + d) % HD
        return pltpu.make_async_remote_copy(
            src_ref=s.at[pl.ds(r0, n), pl.ds(pl.multiple_of(t * W, W), W)],
            dst_ref=dst,
            send_sem=zs.at[j, i],
            recv_sem=zr.at[j, i],
            device_id={"grp": g, "hd": t},
            device_id_type=MESH,
        )

    def own_copy(j):
        s, r0, n, dst = jobs[j]
        return pltpu.make_async_copy(s.at[pl.ds(r0, n), mine], dst, ls.at[j])

    for j in range(len(jobs)):
        own_copy(j).start()
        for i, d in enumerate(Z_ORDER):
            z_copy(j, i, d).start()

    def xy_copy(p, i):
        a, r0, n = IN_PARTS[p]
        r = XY_ORDER[i]
        return pltpu.make_async_remote_copy(
            src_ref=sends[p].at[r],
            dst_ref=got[a].at[opposite(r), pl.ds(r0, n)],
            send_sem=xs.at[p, i],
            recv_sem=xr.at[p, i],
            device_id={"grp": xy_group(g, r), "hd": z},
            device_id_type=MESH,
        )

    def keep_copy(p):
        a, r0, n = IN_PARTS[p]
        return pltpu.make_async_copy(bufs[p], own_out[a].at[:, pl.ds(r0, n)], ls.at[len(jobs) + p])

    for p in range(np_):
        own_copy(p).wait()
        for i, d in enumerate(Z_ORDER):
            z_copy(p, i, d).wait_recv()
        for i, r in enumerate(XY_ORDER):
            sends[p][r] = bufs[p][picked[xy_group(g, r)]]
        for i in range(len(XY_ORDER)):
            xy_copy(p, i).start()
        keep_copy(p).start()
    for j in range(np_, len(jobs)):
        own_copy(j).wait()
        for i, d in enumerate(Z_ORDER):
            z_copy(j, i, d).wait_recv()
    for j in range(len(jobs)):
        for i, d in enumerate(Z_ORDER):
            z_copy(j, i, d).wait_send()
    for p in range(np_):
        keep_copy(p).wait()
        for i in range(len(XY_ORDER)):
            xy_copy(p, i).wait_send()
            xy_copy(p, i).wait_recv()


def gather(picked, q, k, v, do):
    hbm = pl.BlockSpec(memory_space=pl.ANY)
    tile = jax.ShapeDtypeStruct((HD, ROWS, W), BF16)
    slots = jax.ShapeDtypeStruct((GRP, ROWS, W), BF16)
    nj, np_ = len(IN_PARTS) + 2, len(IN_PARTS)
    dma = pltpu.SemaphoreType.DMA
    return pl.pallas_call(
        gather_kernel,
        name="gather",
        out_shape=(tile, tile, tile, tile, slots, slots),
        in_specs=[pl.BlockSpec(memory_space=pltpu.SMEM)] + [hbm] * 4,
        out_specs=(hbm,) * 6,
        scratch_shapes=[pltpu.VMEM((HD, n, W), BF16) for _, _, n in IN_PARTS]
        + [pltpu.VMEM((GRP, n, W), BF16) for _, _, n in IN_PARTS]
        + [dma((nj, 7)), dma((nj, 7)), dma((np_, 31)), dma((np_, 31)), dma((nj + np_,))],
        compiler_params=pltpu.CompilerParams(collective_id=0, has_side_effects=True),
    )(picked, q, k, v, do)


def dot(a, b, ca, cb):
    return lax.dot_general(a, b, (((ca,), (cb,)), ((), ())), preferred_element_type=F32)


def attend_kernel(slot, picked, q, do, ko, vo, kg, vg, att, dq, dko, dvo, bk, bv, order, keep, last, has, acc_k, acc_v, e, ph):
    b = pl.program_id(0)
    nb = 9

    @pl.when(b == 0)
    def _():
        acc_k[...] = jnp.zeros_like(acc_k)
        acc_v[...] = jnp.zeros_like(acc_v)

        def by_block(blk, n):
            has[blk] = 0
            last[blk] = 0
            first = n

            def visit(s, n):
                hit = picked[s] == blk

                @pl.when(hit)
                def _():
                    order[n] = s
                    keep[n] = jnp.where(n == first, 0, 1)
                    last[blk] = n
                    has[blk] = 1

                return n + jnp.where(hit, 1, 0)

            return lax.fori_loop(0, GRP, visit, n)

        used = lax.fori_loop(0, HD, by_block, 0)

        def rest(i, _):
            order[i] = 1
            keep[i] = 0
            return 0

        lax.fori_loop(used, GRP, rest, 0)

    qb, dob = q[0], do[0]
    slots = [None] + [slot[b * 8 + n] for n in range(nb - 1)]

    def key(n):
        return ko[0] if n == 0 else kg[slots[n]]

    def val(n):
        return vo[0] if n == 0 else vg[slots[n]]

    top = None
    for n in range(nb):
        s = dot(key(n), qb, 1, 1)
        e[n] = s
        m = jnp.max(s, axis=0, keepdims=True)
        top = m if top is None else jnp.maximum(top, m)
    total = None
    shift = top * SCALE
    for n in range(nb):
        x = jnp.exp(e[n] * SCALE - shift)
        e[n] = x
        t = jnp.sum(x, axis=0, keepdims=True)
        total = t if total is None else total + t
    inv = 1.0 / total
    out_t = None
    for n in range(nb):
        h = (e[n] * inv).astype(BF16)
        ph[n] = h
        o = dot(val(n), h, 0, 0)
        out_t = o if out_t is None else out_t + o
    delta = jnp.sum(out_t * dob.astype(F32).T, axis=0, keepdims=True)
    att[0] = out_t.T.astype(BF16)
    dq_t = None
    for n in range(nb):
        dp = dot(val(n), dob, 1, 1)
        ds = (e[n] * inv * (dp - delta)).astype(BF16)
        x = dot(key(n), ds, 0, 0)
        dq_t = x if dq_t is None else dq_t + x
        gk = dot(ds, qb, 1, 0)
        gv = dot(ph[n], dob, 1, 0)
        if n == 0:
            dko[0] = gk * SCALE
            dvo[0] = gv
        else:
            acc_k[slots[n]] += gk
            acc_v[slots[n]] += gv
    dq[0] = (dq_t * SCALE).T.astype(BF16)

    @pl.when(b == HD - 1)
    def _():
        def put(s, _):
            bk[s] = (acc_k[s] * SCALE).astype(BF16)
            bv[s] = acc_v[s].astype(BF16)
            return 0

        lax.fori_loop(0, GRP, put, 0)


def attend(slot, picked, qh, doh, kh, vh, kgot, vgot):
    smem = pl.BlockSpec(memory_space=pltpu.SMEM)
    blk = pl.BlockSpec((1, ROWS, W), lambda b: (b, 0, 0))
    whole = pl.BlockSpec(memory_space=pltpu.VMEM)
    tile = jax.ShapeDtypeStruct((HD, ROWS, W), BF16)
    wide = jax.ShapeDtypeStruct((HD, ROWS, W), F32)
    slots = jax.ShapeDtypeStruct((GRP, ROWS, W), BF16)
    table = jax.ShapeDtypeStruct((GRP,), jnp.int32)
    short = jax.ShapeDtypeStruct((HD,), jnp.int32)
    return pl.pallas_call(
        attend_kernel,
        name="attend",
        grid=(HD,),
        out_shape=(tile, tile, wide, wide, slots, slots, table, table, short, short),
        in_specs=[smem, smem, blk, blk, blk, blk, whole, whole],
        out_specs=(blk, blk, blk, blk, whole, whole, smem, smem, smem, smem),
        scratch_shapes=[
            pltpu.VMEM((GRP, ROWS, W), F32),
            pltpu.VMEM((GRP, ROWS, W), F32),
            pltpu.VMEM((9, ROWS, ROWS), F32),
            pltpu.VMEM((9, ROWS, ROWS), BF16),
        ],
        compiler_params=pltpu.CompilerParams(dimension_semantics=("arbitrary",), vmem_limit_bytes=56 << 20),
    )(slot, picked, qh, doh, kh, vh, kgot, vgot)


def give_kernel(order, keep, last, has, att, dq, dko, dvo, bk, bv, out_o, out_q, out_k, out_v, rk, rv0, rv1, run, tk, tv0, tv1, own_k, own_v, zs, zr, xs, xr, ls):
    g, z = lax.axis_index("grp"), lax.axis_index("hd")
    own_loads = [pltpu.make_async_copy(dko, own_k, ls.at[6]), pltpu.make_async_copy(dvo, own_v, ls.at[7])]
    for c in own_loads:
        c.start()
    greet(g, z)
    mine = pl.ds(pl.multiple_of(z * W, W), W)
    src = {"k": bk, "v": bv}
    recv = [rk, rv0, rv1]
    tiles = [tk, tv0, tv1]
    own = {"k": own_k, "v": own_v}
    out = {"k": out_k, "v": out_v}
    jobs = [(att, 0, ROWS, out_o), (dq, 0, ROWS, out_q)]
    jobs += [(tiles[p], r0, n, out[a]) for p, (a, r0, n) in enumerate(OUT_PARTS)]

    def xy_copy(p, i):
        a, r0, n = OUT_PARTS[p]
        r = XY_ORDER[i]
        return pltpu.make_async_remote_copy(
            src_ref=src[a].at[r, pl.ds(r0, n)],
            dst_ref=recv[p].at[opposite(r)],
            send_sem=xs.at[p, i],
            recv_sem=xr.at[p, i],
            device_id={"grp": xy_group(g, r), "hd": z},
            device_id_type=MESH,
        )

    def z_copy(j, i, d):
        s, r0, n, dst = jobs[j]
        t = (z + d) % HD
        return pltpu.make_async_remote_copy(
            src_ref=s.at[t],
            dst_ref=dst.at[pl.ds(r0, n), mine],
            send_sem=zs.at[j, i],
            recv_sem=zr.at[j, i],
            device_id={"grp": g, "hd": t},
            device_id_type=MESH,
        )

    def own_copy(j):
        s, r0, n, dst = jobs[j]
        return pltpu.make_async_copy(s.at[z], dst.at[pl.ds(r0, n), mine], ls.at[j])

    def z_start(j):
        own_copy(j).start()
        for i, d in enumerate(Z_ORDER):
            z_copy(j, i, d).start()

    for i in range(len(XY_ORDER)):
        xy_copy(0, i).start()
    z_start(0)
    for p in range(1, len(OUT_PARTS)):
        for i in range(len(XY_ORDER)):
            xy_copy(p, i).start()
    z_start(1)
    for c in own_loads:
        c.wait()
    for p, (a, r0, n) in enumerate(OUT_PARTS):
        for i in range(len(XY_ORDER)):
            xy_copy(p, i).wait_recv()
        for r1 in range(0, n, 64):
            rows = pl.ds(r1, 64)

            def step(i, acc):
                acc = acc * keep[i].astype(F32) + recv[p][order[i], rows].astype(F32)
                run[i, rows] = acc
                return acc

            lax.fori_loop(0, GRP - 1, step, jnp.zeros((64, W), F32))
        for blk in range(HD):
            extra = run[last[blk], pl.ds(0, n)] * has[blk].astype(F32)
            tiles[p][blk] = (own[a][blk, pl.ds(r0, n)] + extra).astype(BF16)
        z_start(2 + p)
    for j in range(len(jobs)):
        own_copy(j).wait()
        for i, d in enumerate(Z_ORDER):
            z_copy(j, i, d).wait_send()
            z_copy(j, i, d).wait_recv()
    for p in range(len(OUT_PARTS)):
        for i in range(len(XY_ORDER)):
            xy_copy(p, i).wait_send()


def give(tables, att, dq, dko, dvo, bk, bv):
    hbm = pl.BlockSpec(memory_space=pl.ANY)
    flat = jax.ShapeDtypeStruct((ROWS, HD * W), BF16)
    nj, np_ = len(OUT_PARTS) + 2, len(OUT_PARTS)
    dma = pltpu.SemaphoreType.DMA
    return pl.pallas_call(
        give_kernel,
        name="give",
        out_shape=(flat,) * 4,
        in_specs=[pl.BlockSpec(memory_space=pltpu.SMEM)] * 4 + [hbm] * 6,
        out_specs=(hbm,) * 4,
        scratch_shapes=[pltpu.VMEM((GRP, n, W), BF16) for _, _, n in OUT_PARTS]
        + [pltpu.VMEM((GRP, ROWS, W), F32)]
        + [pltpu.VMEM((HD, n, W), BF16) for _, _, n in OUT_PARTS]
        + [pltpu.VMEM((HD, ROWS, W), F32)] * 2
        + [dma((nj, 7)), dma((nj, 7)), dma((np_, 31)), dma((np_, 31)), dma((nj + 3,))],
        compiler_params=pltpu.CompilerParams(collective_id=1, has_side_effects=True),
    )(*tables, att, dq, dko, dvo, bk, bv)


def on_device(queries, keys, values, grad_out, neighbours):
    g = lax.axis_index("grp")
    listed = neighbours.reshape(GRP, -1)
    picked = jnp.max(jnp.where(listed // HD == g, listed % HD, -1), axis=1)
    own = lax.dynamic_slice_in_dim(listed, g, 1, axis=0)[0] // HD
    dy = (own // 8 - g // 8) % 4
    dx = ((own // 2) % 4 - (g // 2) % 4) % 4
    dc = (own % 2 - g % 2) % 2
    slot = dy * 8 + dx * 2 + dc
    places = jnp.arange(GRP, dtype=jnp.int32)
    r_group = (((g // 8 + places // 8) % 4) * 4 + ((g // 2) % 4 + (places // 2) % 4) % 4) * 2 + (g % 2 + places % 2) % 2
    hit = jnp.where(listed[None] // HD == g, listed[None] % HD, -1)
    picked_r = jnp.max(jnp.where((r_group[:, None] == places[None, :])[:, :, None], hit, -1), axis=(1, 2))
    qh, kh, vh, doh, kgot, vgot = gather(jnp.maximum(picked, 0), queries, keys, values, grad_out)
    att, dq, dko, dvo, bk, bv, *tables = attend(slot, picked_r, qh, doh, kh, vh, kgot, vgot)
    return tuple(give(tables, att, dq, dko, dvo, bk, bv))


def solution(mesh):
    part = P(("grp", "hd"), None)
    return jax.shard_map(
        on_device, mesh=mesh, in_specs=(part,) * 4 + (P(),), out_specs=(part,) * 4, check_vma=False
    )
```

```python
import jax
import jax.numpy as jnp
from jax import lax
from jax.experimental import pallas as pl
from jax.experimental.pallas import tpu as pltpu
from jax.sharding import PartitionSpec as P

MESH = pl.DeviceIdType.MESH
HD = 8
GRP = 32
ROWS = 256
W = 128
F32 = jnp.float32
BF16 = jnp.bfloat16
SCALE = W ** (-0.5)

PLACES = [(0, 1), (1, 0), (0, 3), (3, 0), (0, 2), (2, 0), (1, 1), (3, 3), (1, 3), (3, 1), (2, 2), (1, 2), (2, 1), (3, 2), (2, 3), (0, 0)]
XY_ORDER = [dy * 8 + dx * 2 + dc for dc in (0, 1) for dy, dx in PLACES if dy + dx + dc > 0]
Z_ORDER = [1, 7, 2, 6, 3, 5, 4]


def opposite(r):
    return ((4 - r // 8) % 4) * 8 + ((4 - (r // 2) % 4) % 4) * 2 + r % 2


def xy_group(g, r):
    c, x, y = g % 2, (g // 2) % 4, g // 8
    return (((y + r // 8) % 4) * 4 + (x + (r // 2) % 4) % 4) * 2 + (c + r % 2) % 2


def greet(g, z):
    barrier = pltpu.get_barrier_semaphore()
    for r in XY_ORDER:
        pl.semaphore_signal(barrier, inc=1, device_id={"grp": xy_group(g, r), "hd": z}, device_id_type=MESH)
    for d in Z_ORDER:
        pl.semaphore_signal(barrier, inc=1, device_id={"grp": g, "hd": (z + d) % HD}, device_id_type=MESH)
    pl.semaphore_wait(barrier, len(XY_ORDER) + len(Z_ORDER))


HALF = ROWS // 2
NB = 8
PAIRS = HD * NB

PICKED, SLOT, LISTER, FILL, ORDER, KEEP, LAST, HAS, END = 0, 32, 96, 224, 256, 288, 320, 328, 336


def dot(a, b, ca, cb):
    return lax.dot_general(a, b, (((ca,), (cb,)), ((), ())), preferred_element_type=F32)


def kernel(tab, q, k, v, do, out_o, out_q, out_k, out_v, *scr):
    (k0, k1, vv, qh, doh, sk0, sk1, sv, gk0, gk1, gv, probs, pair, own_k, own_v, give_v, give_k, back_v, back_k0, back_k1, run, att, dq,
     tv, tk0, tk1, zs, zr, xs, xr, ls) = scr
    g, z = lax.axis_index("grp"), lax.axis_index("hd")
    mine = pl.ds(pl.multiple_of(z * W, W), W)
    nxy = len(XY_ORDER)
    inward = [(k, 0, HALF, k0), (k, HALF, HALF, k1), (v, 0, ROWS, vv), (q, 0, ROWS, qh), (do, 0, ROWS, doh)]
    outward = [(att, 0, ROWS, out_o), (dq, 0, ROWS, out_q), (tv, 0, ROWS, out_v), (tk0, 0, HALF, out_k), (tk1, HALF, HALF, out_k)]
    across = [(sk0, 0, HALF, gk0), (sk1, 0, HALF, gk1), (sv, 0, ROWS, gv)]
    across += [(give_v, 0, ROWS, back_v), (give_k, 0, HALF, back_k0), (give_k, HALF, HALF, back_k1)]
    nin = len(inward)

    def z_copy(j, i):
        d = Z_ORDER[i]
        t = (z + d) % HD
        if j < nin:
            s, r0, n, to = inward[j]
            src, dst = s.at[pl.ds(r0, n), pl.ds(pl.multiple_of(t * W, W), W)], to.at[z]
        else:
            s, r0, n, to = outward[j - nin]
            src, dst = s.at[t], to.at[pl.ds(r0, n), mine]
        return pltpu.make_async_remote_copy(
            src_ref=src, dst_ref=dst, send_sem=zs.at[j, i], recv_sem=zr.at[j, i],
            device_id={"grp": g, "hd": t}, device_id_type=MESH,
        )

    def own_copy(j):
        if j < nin:
            s, r0, n, to = inward[j]
            return pltpu.make_async_copy(s.at[pl.ds(r0, n), mine], to.at[z], ls.at[j])
        s, r0, n, to = outward[j - nin]
        return pltpu.make_async_copy(s.at[z], to.at[pl.ds(r0, n), mine], ls.at[j])

    def z_start(j):
        own_copy(j).start()
        for i in range(len(Z_ORDER)):
            z_copy(j, i).start()

    def z_arrive(j):
        own_copy(j).wait()
        for i in range(len(Z_ORDER)):
            z_copy(j, i).wait_recv()

    def xy_copy(p, i):
        s, r0, n, to = across[p]
        r = XY_ORDER[i]
        return pltpu.make_async_remote_copy(
            src_ref=s.at[r, pl.ds(r0, n)], dst_ref=to.at[opposite(r)],
            send_sem=xs.at[p, i], recv_sem=xr.at[p, i],
            device_id={"grp": xy_group(g, r), "hd": z}, device_id_type=MESH,
        )

    def xy_start(p):
        for i in range(nxy):
            xy_copy(p, i).start()

    def xy_arrive(p):
        for i in range(nxy):
            xy_copy(p, i).wait_recv()

    greet(g, z)
    for j in range(nin):
        z_start(j)
    for p, buf in enumerate((k0, k1, vv)):
        z_arrive(p)
        for r in XY_ORDER:
            across[p][0][r] = buf[tab[PICKED + xy_group(g, r)]]
        xy_start(p)
    z_arrive(3)
    z_arrive(4)
    xy_arrive(0)
    xy_arrive(1)

    def slots_of(b):
        return [None] + [tab[SLOT + b * NB + n] for n in range(NB)]

    def keys_of(b, slots, n):
        if n == 0:
            return jnp.concatenate([k0[b], k1[b]], axis=0)
        return jnp.concatenate([gk0[slots[n]], gk1[slots[n]]], axis=0)

    def values_of(b, slots, n):
        return vv[b] if n == 0 else gv[slots[n]]

    def first_half(b, _):
        slots = slots_of(b)
        qb, dob = qh[b], doh[b]
        top = None
        scores = []
        for n in range(NB + 1):
            s = dot(keys_of(b, slots, n), qb, 1, 1)
            run[n // 2, :, pl.ds((n % 2) * ROWS, ROWS)] = s
            m = jnp.max(s, axis=0, keepdims=True)
            top = m if top is None else jnp.maximum(top, m)
        shift = top * SCALE
        total = None
        for n in range(NB + 1):
            at = (n // 2, slice(None), pl.ds((n % 2) * ROWS, ROWS))
            x = jnp.exp(run[at] * SCALE - shift)
            run[at] = x
            t = jnp.sum(x, axis=0, keepdims=True)
            total = t if total is None else total + t
        inv = 1.0 / total
        for n in range(NB + 1):
            h = (run[n // 2, :, pl.ds((n % 2) * ROWS, ROWS)] * inv).astype(BF16)
            probs[b, n] = h
            x = dot(h, dob, 1, 0)
            if n == 0:
                own_v[b] = x
            else:
                pair[b * NB + n - 1] = x
        return 0

    lax.fori_loop(0, HD, first_half, 0)

    def collect(to, scale):
        def one(r, _):
            f = tab[FILL + r].astype(F32) * scale
            for r0 in range(0, ROWS, HALF):
                rows = pl.ds(r0, HALF)
                x = pair[tab[LISTER + r * 4], rows]
                for m in range(1, 4):
                    x = x + pair[tab[LISTER + r * 4 + m], rows]
                to[r, rows] = (x * f).astype(BF16)
            return 0

        lax.fori_loop(1, GRP, one, 0)

    collect(give_v, 1.0)
    xy_start(3)
    xy_arrive(2)

    def second_half(b, _):
        slots = slots_of(b)
        qb, dob = qh[b], doh[b]
        out_t = None
        for n in range(NB + 1):
            o = dot(values_of(b, slots, n), probs[b, n], 0, 0)
            out_t = o if out_t is None else out_t + o
        delta = jnp.sum(out_t * dob.astype(F32).T, axis=0, keepdims=True)
        att[b] = out_t.T.astype(BF16)
        dq_t = None
        for n in range(NB + 1):
            dp = dot(values_of(b, slots, n), dob, 1, 1)
            ds = (probs[b, n].astype(F32) * (dp - delta)).astype(BF16)
            x = dot(keys_of(b, slots, n), ds, 0, 0)
            dq_t = x if dq_t is None else dq_t + x
            x = dot(ds, qb, 1, 0)
            if n == 0:
                own_k[b] = x * SCALE
            else:
                pair[b * NB + n - 1] = x
        dq[b] = (dq_t * SCALE).T.astype(BF16)
        return 0

    lax.fori_loop(0, HD, second_half, 0)
    collect(give_k, SCALE)
    xy_start(4)
    xy_start(5)
    z_start(nin)
    z_start(nin + 1)
    totals = [(3, back_v, own_v, tv, 0, ROWS), (4, back_k0, own_k, tk0, 0, HALF), (5, back_k1, own_k, tk1, HALF, HALF)]
    for i, (p, back, own, tile, r0, n) in enumerate(totals):
        xy_arrive(p)
        for r1 in range(0, n, 64):
            rows = pl.ds(r1, 64)

            def step(m, acc):
                acc = acc * tab[KEEP + m].astype(F32) + back[tab[ORDER + m], rows].astype(F32)
                pair[m, rows] = acc
                return acc

            lax.fori_loop(0, GRP - 1, step, jnp.zeros((64, W), F32))
        for blk in range(HD):
            extra = pair[tab[LAST + blk], pl.ds(0, n)] * tab[HAS + blk].astype(F32)
            tile[blk] = (own[blk, pl.ds(r0, n)] + extra).astype(BF16)
        z_start(nin + 2 + i)
    for j in range(nin, nin + len(outward)):
        z_arrive(j)
    for j in range(nin + len(outward)):
        for i in range(len(Z_ORDER)):
            z_copy(j, i).wait_send()
    for p in range(len(across)):
        for i in range(nxy):
            xy_copy(p, i).wait_send()


def run_kernel(tab, q, k, v, do):
    hbm = pl.BlockSpec(memory_space=pl.ANY)
    flat = jax.ShapeDtypeStruct((ROWS, HD * W), BF16)
    dma = pltpu.SemaphoreType.DMA

    def tiles(n, rows=ROWS, dtype=BF16):
        return pltpu.VMEM((n, rows, W), dtype)

    return pl.pallas_call(
        kernel,
        name="graph_attention",
        out_shape=(flat,) * 4,
        in_specs=[pl.BlockSpec(memory_space=pltpu.SMEM)] + [hbm] * 4,
        out_specs=(hbm,) * 4,
        scratch_shapes=[
            tiles(HD, HALF), tiles(HD, HALF), tiles(HD), tiles(HD), tiles(HD),
            tiles(GRP, HALF), tiles(GRP, HALF), tiles(GRP), tiles(GRP, HALF), tiles(GRP, HALF), tiles(GRP),
            pltpu.VMEM((HD, NB + 1, ROWS, ROWS), BF16),
            tiles(PAIRS, ROWS, F32), tiles(HD, ROWS, F32), tiles(HD, ROWS, F32),
            tiles(GRP), tiles(GRP), tiles(GRP), tiles(GRP, HALF), tiles(GRP, HALF),
            pltpu.VMEM((5, ROWS, 2 * ROWS), F32),
            tiles(HD), tiles(HD), tiles(HD), tiles(HD, HALF), tiles(HD, HALF),
            dma((10, 7)), dma((10, 7)), dma((6, 31)), dma((6, 31)), dma((10,)),
        ],
        compiler_params=pltpu.CompilerParams(collective_id=0, has_side_effects=True, vmem_limit_bytes=62 << 20),
    )(tab, q, k, v, do)


def tables(neighbours):
    g = lax.axis_index("grp")
    listed = neighbours.reshape(GRP, -1)
    picked = jnp.max(jnp.where(listed // HD == g, listed % HD, -1), axis=1)
    places = jnp.arange(GRP, dtype=jnp.int32)
    r_group = xy_group(g, places)
    own = lax.dynamic_slice_in_dim(listed, g, 1, axis=0)[0] // HD
    slot = ((own // 8 - g // 8) % 4) * 8 + ((own // 2 - g // 2) % 4) * 2 + (own - g) % 2
    index = jnp.arange(PAIRS, dtype=jnp.int32)
    rank = jnp.sum((own[None, :] == own[:, None]) & (index[None, :] < index[:, None]), axis=1)
    mark = jnp.where(slot[None, :] == places[:, None], rank[None, :], -1)
    lister = jnp.max(jnp.where(mark[:, None, :] == jnp.arange(4)[None, :, None], index[None, None, :], 0), axis=2)
    fill = jnp.max(jnp.where(mark >= 0, 1, 0), axis=1)
    mine = jnp.max(jnp.where(r_group[:, None] == places[None, :], picked[None, :], -1), axis=1)
    block = jnp.where(places == 0, HD + 1, jnp.where(mine < 0, HD, mine))
    sort = block * GRP + places
    pos = jnp.sum(sort[None, :] < sort[:, None], axis=1)
    at = pos[None, :] == places[:, None]
    order = jnp.sum(jnp.where(at, places[None, :], 0), axis=1)
    sorted_block = jnp.sum(jnp.where(at, block[None, :], 0), axis=1)
    keep = jnp.sum(jnp.where((pos[None, :] + 1 == places[:, None]) & (block[None, :] == sorted_block[:, None]), 1, 0), axis=1)
    blocks = jnp.arange(HD, dtype=jnp.int32)
    upto = jnp.sum(block[None, :] <= blocks[:, None], axis=1)
    has = jnp.max(jnp.where(block[None, :] == blocks[:, None], 1, 0), axis=1)
    parts = [jnp.maximum(picked, 0), slot, lister.reshape(-1), fill, order, keep, jnp.maximum(upto - 1, 0), has]
    return jnp.concatenate([x.astype(jnp.int32) for x in parts])


def on_device(queries, keys, values, grad_out, neighbours):
    return tuple(run_kernel(tables(neighbours), queries, keys, values, grad_out))


def solution(mesh):
    part = P(("grp", "hd"), None)
    return jax.shard_map(
        on_device, mesh=mesh, in_specs=(part,) * 4 + (P(),), out_specs=(part,) * 4, check_vma=False
    )
```

```python
import jax
import jax.numpy as jnp
from jax import lax
from jax.experimental import pallas as pl
from jax.experimental.pallas import tpu as pltpu
from jax.sharding import PartitionSpec as P

MESH = pl.DeviceIdType.MESH
HD = 8
GRP = 32
ROWS = 256
W = 128
F32 = jnp.float32
BF16 = jnp.bfloat16
SCALE = W ** (-0.5)

PLACES = [(0, 1), (1, 0), (0, 3), (3, 0), (0, 2), (2, 0), (1, 1), (3, 3), (1, 3), (3, 1), (2, 2), (1, 2), (2, 1), (3, 2), (2, 3), (0, 0)]
XY_ORDER = [dy * 8 + dx * 2 + dc for dc in (0, 1) for dy, dx in PLACES if dy + dx + dc > 0]
Z_ORDER = [1, 7, 2, 6, 3, 5, 4]


def z_dist(i):
    return jnp.where(i == 7, 0, jnp.where(i % 2 == 0, i // 2 + 1, 7 - i // 2))


def opposite(r):
    return ((4 - r // 8) % 4) * 8 + ((4 - (r // 2) % 4) % 4) * 2 + r % 2


def xy_group(g, r):
    c, x, y = g % 2, (g // 2) % 4, g // 8
    return (((y + r // 8) % 4) * 4 + (x + (r // 2) % 4) % 4) * 2 + (c + r % 2) % 2


def greet(g, z):
    barrier = pltpu.get_barrier_semaphore()
    for r in XY_ORDER:
        pl.semaphore_signal(barrier, inc=1, device_id={"grp": xy_group(g, r), "hd": z}, device_id_type=MESH)
    for d in Z_ORDER:
        pl.semaphore_signal(barrier, inc=1, device_id={"grp": g, "hd": (z + d) % HD}, device_id_type=MESH)
    pl.semaphore_wait(barrier, len(XY_ORDER) + len(Z_ORDER))


HALF = ROWS // 2
NB = 8
PAIRS = HD * NB

PICKED, SLOT, LISTER, FILL, ORDER, KEEP, LAST, HAS, END = 0, 32, 96, 224, 256, 288, 320, 328, 336


def dot(a, b, ca, cb):
    return lax.dot_general(a, b, (((ca,), (cb,)), ((), ())), preferred_element_type=F32)


def kernel(tab, q, k, v, do, out_o, out_q, out_k, out_v, *scr):
    (k0, k1, vv, qh, doh, sk0, sk1, sv, gk0, gk1, gv, probs, pair, own_k, own_v, give_v, give_k, back_v, back_k0, back_k1, run, att, dq,
     tv, tk0, tk1, zs, zr, xs, xr, ls) = scr
    g, z = lax.axis_index("grp"), lax.axis_index("hd")
    mine = pl.ds(pl.multiple_of(z * W, W), W)
    nxy = len(XY_ORDER)
    inward = [(k, 0, HALF, k0), (k, HALF, HALF, k1), (v, 0, ROWS, vv), (q, 0, ROWS, qh), (do, 0, ROWS, doh)]
    outward = [(att, 0, ROWS, out_o), (dq, 0, ROWS, out_q), (tv, 0, ROWS, out_v), (tk0, 0, HALF, out_k), (tk1, HALF, HALF, out_k)]
    across = [(sk0, 0, HALF, gk0), (sk1, 0, HALF, gk1), (sv, 0, ROWS, gv)]
    across += [(give_v, 0, ROWS, back_v), (give_k, 0, HALF, back_k0), (give_k, HALF, HALF, back_k1)]
    nin = len(inward)

    def z_copy(j, i):
        t = (z + (Z_ORDER[i] if isinstance(i, int) else z_dist(i))) % HD
        if j < nin:
            s, r0, n, to = inward[j]
            src, dst = s.at[pl.ds(r0, n), pl.ds(pl.multiple_of(t * W, W), W)], to.at[z]
        else:
            s, r0, n, to = outward[j - nin]
            src, dst = s.at[t], to.at[z, pl.ds(r0, n)]
        return pltpu.make_async_remote_copy(
            src_ref=src, dst_ref=dst, send_sem=zs.at[j, i], recv_sem=zr.at[j, i],
            device_id={"grp": g, "hd": t}, device_id_type=MESH,
        )

    def own_copy(j):
        if j < nin:
            s, r0, n, to = inward[j]
            return pltpu.make_async_copy(s.at[pl.ds(r0, n), mine], to.at[z], ls.at[j])
        s, r0, n, to = outward[j - nin]
        return pltpu.make_async_copy(s.at[z], to.at[z, pl.ds(r0, n)], ls.at[j])

    def z_start(j):
        own_copy(j).start()
        for i in range(len(Z_ORDER)):
            z_copy(j, i).start()

    def z_arrive(j):
        own_copy(j).wait()
        for i in range(len(Z_ORDER)):
            z_copy(j, i).wait_recv()

    def xy_copy(p, i):
        s, r0, n, to = across[p]
        r = XY_ORDER[i]
        return pltpu.make_async_remote_copy(
            src_ref=s.at[r, pl.ds(r0, n)], dst_ref=to.at[opposite(r)],
            send_sem=xs.at[p, i], recv_sem=xr.at[p, i],
            device_id={"grp": xy_group(g, r), "hd": z}, device_id_type=MESH,
        )

    def xy_start(p):
        for i in range(nxy):
            xy_copy(p, i).start()

    def xy_arrive(p):
        for i in range(nxy):
            xy_copy(p, i).wait_recv()

    greet(g, z)
    for j in range(nin):
        z_start(j)
    for p, buf in enumerate((k0, k1, vv)):
        z_arrive(p)
        for r in XY_ORDER:
            across[p][0][r] = buf[tab[PICKED + xy_group(g, r)]]
        xy_start(p)
    z_arrive(3)
    xy_arrive(0)
    xy_arrive(1)

    def slots_of(b):
        return [None] + [tab[SLOT + b * NB + n] for n in range(NB)]

    def keys_of(b, slots, n):
        if n == 0:
            return jnp.concatenate([k0[b], k1[b]], axis=0)
        return jnp.concatenate([gk0[slots[n]], gk1[slots[n]]], axis=0)

    def values_of(b, slots, n):
        return vv[b] if n == 0 else gv[slots[n]]

    def first_half(b, _):
        slots = slots_of(b)
        qb = qh[b]
        top = None
        scores = []
        for n in range(NB + 1):
            s = dot(keys_of(b, slots, n), qb, 1, 1)
            run[n // 2, :, pl.ds((n % 2) * ROWS, ROWS)] = s
            m = jnp.max(s, axis=0, keepdims=True)
            top = m if top is None else jnp.maximum(top, m)
        shift = top * SCALE
        total = None
        for n in range(NB + 1):
            at = (n // 2, slice(None), pl.ds((n % 2) * ROWS, ROWS))
            x = jnp.exp(run[at] * SCALE - shift)
            run[at] = x
            t = jnp.sum(x, axis=0, keepdims=True)
            total = t if total is None else total + t
        inv = 1.0 / total
        for n in range(NB + 1):
            probs[b, n] = (run[n // 2, :, pl.ds((n % 2) * ROWS, ROWS)] * inv).astype(BF16)
        return 0

    lax.fori_loop(0, HD, first_half, 0)
    z_arrive(4)

    def value_grads(b, _):
        dob = doh[b]
        for n in range(NB + 1):
            x = dot(probs[b, n], dob, 1, 0)
            if n == 0:
                own_v[b] = x
            else:
                pair[b * NB + n - 1] = x
        return 0

    lax.fori_loop(0, HD, value_grads, 0)

    def collect(to, scale):
        def one(r, _):
            f = tab[FILL + r].astype(F32) * scale
            for r0 in range(0, ROWS, HALF):
                rows = pl.ds(r0, HALF)
                x = pair[tab[LISTER + r * 4], rows]
                for m in range(1, 4):
                    x = x + pair[tab[LISTER + r * 4 + m], rows]
                to[r, rows] = (x * f).astype(BF16)
            return 0

        lax.fori_loop(1, GRP, one, 0)

    collect(give_v, 1.0)
    xy_start(3)
    xy_arrive(2)

    def z_send(j, i):
        @pl.when(i < 7)
        def _():
            z_copy(j, i).start()

        @pl.when(i == 7)
        def _():
            own_copy(j).start()

    def second_half(i, _):
        b = (z + z_dist(i)) % HD
        slots = slots_of(b)
        qb, dob = qh[b], doh[b]
        out_t = None
        for n in range(NB + 1):
            o = dot(values_of(b, slots, n), probs[b, n], 0, 0)
            out_t = o if out_t is None else out_t + o
        delta = jnp.sum(out_t * dob.astype(F32).T, axis=0, keepdims=True)
        att[b] = out_t.T.astype(BF16)
        z_send(nin, i)
        dq_t = None
        for n in range(NB + 1):
            dp = dot(values_of(b, slots, n), dob, 1, 1)
            ds = (probs[b, n].astype(F32) * (dp - delta)).astype(BF16)
            x = dot(keys_of(b, slots, n), ds, 0, 0)
            dq_t = x if dq_t is None else dq_t + x
            x = dot(ds, qb, 1, 0)
            if n == 0:
                own_k[b] = x * SCALE
            else:
                pair[b * NB + n - 1] = x
        dq[b] = (dq_t * SCALE).T.astype(BF16)
        z_send(nin + 1, i)
        return 0

    lax.fori_loop(0, HD, second_half, 0)
    collect(give_k, SCALE)
    xy_start(4)
    xy_start(5)
    totals = [(3, back_v, own_v, tv, 0, ROWS), (4, back_k0, own_k, tk0, 0, HALF), (5, back_k1, own_k, tk1, HALF, HALF)]
    for i, (p, back, own, tile, r0, n) in enumerate(totals):
        xy_arrive(p)
        for r1 in range(0, n, 64):
            rows = pl.ds(r1, 64)

            def step(m, acc):
                acc = acc * tab[KEEP + m].astype(F32) + back[tab[ORDER + m], rows].astype(F32)
                pair[m, rows] = acc
                return acc

            lax.fori_loop(0, GRP - 1, step, jnp.zeros((64, W), F32))
        for blk in range(HD):
            extra = pair[tab[LAST + blk], pl.ds(0, n)] * tab[HAS + blk].astype(F32)
            tile[blk] = (own[blk, pl.ds(r0, n)] + extra).astype(BF16)
        z_start(nin + 2 + i)
    for j in range(nin, nin + len(outward)):
        z_arrive(j)
    for j in range(nin + len(outward)):
        for i in range(len(Z_ORDER)):
            z_copy(j, i).wait_send()
    for p in range(len(across)):
        for i in range(nxy):
            xy_copy(p, i).wait_send()


def run_kernel(tab, q, k, v, do):
    hbm = pl.BlockSpec(memory_space=pl.ANY)
    by_head = jax.ShapeDtypeStruct((HD, ROWS, W), BF16)
    dma = pltpu.SemaphoreType.DMA

    def tiles(n, rows=ROWS, dtype=BF16):
        return pltpu.VMEM((n, rows, W), dtype)

    return pl.pallas_call(
        kernel,
        name="graph_attention",
        out_shape=(by_head,) * 4,
        in_specs=[pl.BlockSpec(memory_space=pltpu.SMEM)] + [hbm] * 4,
        out_specs=(hbm,) * 4,
        scratch_shapes=[
            tiles(HD, HALF), tiles(HD, HALF), tiles(HD), tiles(HD), tiles(HD),
            tiles(GRP, HALF), tiles(GRP, HALF), tiles(GRP), tiles(GRP, HALF), tiles(GRP, HALF), tiles(GRP),
            pltpu.VMEM((HD, NB + 1, ROWS, ROWS), BF16),
            tiles(PAIRS, ROWS, F32), tiles(HD, ROWS, F32), tiles(HD, ROWS, F32),
            tiles(GRP), tiles(GRP), tiles(GRP), tiles(GRP, HALF), tiles(GRP, HALF),
            pltpu.VMEM((5, ROWS, 2 * ROWS), F32),
            tiles(HD), tiles(HD), tiles(HD), tiles(HD, HALF), tiles(HD, HALF),
            dma((10, 7)), dma((10, 7)), dma((6, 31)), dma((6, 31)), dma((10,)),
        ],
        compiler_params=pltpu.CompilerParams(collective_id=0, has_side_effects=True, vmem_limit_bytes=62 << 20),
    )(tab, q, k, v, do)


def lay_kernel(*refs):
    for src, dst in zip(refs[:4], refs[4:]):
        for h in range(HD):
            dst[:, h * W : (h + 1) * W] = src[h]


def lay(tiles):
    steps = 4
    rows = ROWS // steps
    return pl.pallas_call(
        lay_kernel,
        name="lay",
        grid=(steps,),
        out_shape=(jax.ShapeDtypeStruct((ROWS, HD * W), BF16),) * 4,
        in_specs=[pl.BlockSpec((HD, rows, W), lambda i: (0, i, 0))] * 4,
        out_specs=(pl.BlockSpec((rows, HD * W), lambda i: (i, 0)),) * 4,
        compiler_params=pltpu.CompilerParams(dimension_semantics=("arbitrary",), vmem_limit_bytes=62 << 20),
    )(*tiles)


def tables(neighbours):
    g = lax.axis_index("grp")
    listed = neighbours.reshape(GRP, -1)
    picked = jnp.max(jnp.where(listed // HD == g, listed % HD, -1), axis=1)
    places = jnp.arange(GRP, dtype=jnp.int32)
    r_group = xy_group(g, places)
    own = lax.dynamic_slice_in_dim(listed, g, 1, axis=0)[0] // HD
    slot = ((own // 8 - g // 8) % 4) * 8 + ((own // 2 - g // 2) % 4) * 2 + (own - g) % 2
    index = jnp.arange(PAIRS, dtype=jnp.int32)
    rank = jnp.sum((own[None, :] == own[:, None]) & (index[None, :] < index[:, None]), axis=1)
    mark = jnp.where(slot[None, :] == places[:, None], rank[None, :], -1)
    lister = jnp.max(jnp.where(mark[:, None, :] == jnp.arange(4)[None, :, None], index[None, None, :], 0), axis=2)
    fill = jnp.max(jnp.where(mark >= 0, 1, 0), axis=1)
    mine = jnp.max(jnp.where(r_group[:, None] == places[None, :], picked[None, :], -1), axis=1)
    block = jnp.where(places == 0, HD + 1, jnp.where(mine < 0, HD, mine))
    sort = block * GRP + places
    pos = jnp.sum(sort[None, :] < sort[:, None], axis=1)
    at = pos[None, :] == places[:, None]
    order = jnp.sum(jnp.where(at, places[None, :], 0), axis=1)
    sorted_block = jnp.sum(jnp.where(at, block[None, :], 0), axis=1)
    keep = jnp.sum(jnp.where((pos[None, :] + 1 == places[:, None]) & (block[None, :] == sorted_block[:, None]), 1, 0), axis=1)
    blocks = jnp.arange(HD, dtype=jnp.int32)
    upto = jnp.sum(block[None, :] <= blocks[:, None], axis=1)
    has = jnp.max(jnp.where(block[None, :] == blocks[:, None], 1, 0), axis=1)
    parts = [jnp.maximum(picked, 0), slot, lister.reshape(-1), fill, order, keep, jnp.maximum(upto - 1, 0), has]
    return jnp.concatenate([x.astype(jnp.int32) for x in parts])


def on_device(queries, keys, values, grad_out, neighbours):
    return tuple(lay(run_kernel(tables(neighbours), queries, keys, values, grad_out)))


def solution(mesh):
    part = P(("grp", "hd"), None)
    return jax.shard_map(
        on_device, mesh=mesh, in_specs=(part,) * 4 + (P(),), out_specs=(part,) * 4, check_vma=False
    )
```

```python
import jax
import jax.numpy as jnp
from jax import lax
from jax.experimental import pallas as pl
from jax.experimental.pallas import tpu as pltpu
from jax.sharding import PartitionSpec as P

MESH = pl.DeviceIdType.MESH
HD = 8
GRP = 32
ROWS = 256
W = 128
F32 = jnp.float32
BF16 = jnp.bfloat16
SCALE = W ** (-0.5)

PLACES = [(0, 1), (1, 0), (0, 3), (3, 0), (0, 2), (2, 0), (1, 1), (3, 3), (1, 3), (3, 1), (2, 2), (1, 2), (2, 1), (3, 2), (2, 3), (0, 0)]
XY_ORDER = [dy * 8 + dx * 2 + dc for dc in (0, 1) for dy, dx in PLACES if dy + dx + dc > 0]
Z_ORDER = [1, 7, 2, 6, 3, 5, 4]


def z_dist(i):
    return jnp.where(i == 7, 0, jnp.where(i % 2 == 0, i // 2 + 1, 7 - i // 2))


def opposite(r):
    return ((4 - r // 8) % 4) * 8 + ((4 - (r // 2) % 4) % 4) * 2 + r % 2


def xy_group(g, r):
    c, x, y = g % 2, (g // 2) % 4, g // 8
    return (((y + r // 8) % 4) * 4 + (x + (r // 2) % 4) % 4) * 2 + (c + r % 2) % 2


def greet(g, z):
    barrier = pltpu.get_barrier_semaphore()
    for r in XY_ORDER:
        pl.semaphore_signal(barrier, inc=1, device_id={"grp": xy_group(g, r), "hd": z}, device_id_type=MESH)
    for d in Z_ORDER:
        pl.semaphore_signal(barrier, inc=1, device_id={"grp": g, "hd": (z + d) % HD}, device_id_type=MESH)


def met():
    pl.semaphore_wait(pltpu.get_barrier_semaphore(), len(XY_ORDER) + len(Z_ORDER))


NB = 8
PAIRS = HD * NB

INWARD = [("k", 0, 48), ("k", 48, 80), ("k", 128, 128), ("v", 0, 128), ("q", 0, 256), ("v", 128, 128), ("do", 0, 256)]
LISTED = [i for i, part in enumerate(INWARD) if part[0] in "kv"]
RETURN = [("v", 0, 128), ("v", 128, 128), ("k", 0, 128), ("k", 128, 64), ("k", 192, 64)]
NIN, NLIST, NRET = len(INWARD), len(LISTED), len(RETURN)

PICKED, LISTER, FILL, ORDER, KEEP, LAST, HAS = 0, 1, 5, 6, 7, 8, 9
SLOT_ROW = 32


def dot(a, b, ca, cb):
    return lax.dot_general(a, b, (((ca,), (cb,)), ((), ())), preferred_element_type=F32)


def index_table(g, lists, table):
    def iota(shape, dim):
        return lax.broadcasted_iota(jnp.int32, shape, dim)

    def down(x):
        return jnp.sum(x, axis=0, keepdims=True)

    def along(x):
        return jnp.sum(x, axis=1, keepdims=True)

    def most(x):
        return jnp.max(x, axis=1, keepdims=True)

    def ones(cond):
        return jnp.where(cond, 1, 0)

    def as_row(col):
        n = col.shape[0]
        return down(jnp.where(iota((n, n), 0) == iota((n, n), 1), col, 0))

    def place_of(blk):
        other = blk // HD
        dy = (other // 8 - g // 8 + 4) % 4
        dx = ((other // 2) % 4 - (g // 2) % 4 + 4) % 4
        return dy * 8 + dx * 2 + (other % 2 - g % 2 + 2) % 2

    nb = lists[...]
    best = jnp.max(jnp.where(nb // HD == g, nb % HD, -1), axis=0, keepdims=True)
    place = iota((GRP, 1), 0)
    by = iota((GRP, GRP * HD), 1) // HD
    picked = most(jnp.where(by == iota((GRP, GRP * HD), 0), best, -1))
    mine = most(jnp.where(by == xy_group(g, place), best, -1))
    lane = iota((NB, GRP * HD), 1)
    own = jnp.concatenate([along(jnp.where(lane == g * HD + b, nb, 0)) for b in range(HD)], axis=0)
    slot_col, slot_row = place_of(own), place_of(as_row(own))
    s64, l64 = iota((PAIRS, PAIRS), 0), iota((PAIRS, PAIRS), 1)
    rank = down(ones((slot_col == slot_row) & (s64 < l64)))
    mark = jnp.where(slot_row == iota((GRP, PAIRS), 0), rank, -1)
    lister = [most(jnp.where(mark == m, iota((GRP, PAIRS), 1), 0)) for m in range(4)]
    fill = most(ones(mark >= 0))
    s32, l32 = iota((GRP, GRP), 0), iota((GRP, GRP), 1)
    block = jnp.where(place == 0, HD + 1, jnp.where(mine < 0, HD, mine))
    block_row = as_row(block)
    key = block * GRP + place
    pos = down(ones(key < as_row(key)))
    at = pos == s32
    order = along(jnp.where(at, l32, 0))
    sorted_block = along(jnp.where(at, block_row, 0))
    keep = along(ones((pos + 1 == s32) & (block_row == sorted_block)))
    last = along(ones(block_row <= s32)) - 1
    has = most(ones(block_row == s32))
    cols = [jnp.maximum(picked, 0)] + lister + [fill, order, keep, jnp.maximum(last, 0), has]
    out = jnp.zeros((GRP, W), jnp.int32)
    for c, col in enumerate(cols):
        out = jnp.where(iota((GRP, W), 1) == c, col, out)
    table[pl.ds(0, GRP)] = out
    slots = jnp.concatenate([slot_row, jnp.zeros((1, W - PAIRS), jnp.int32)], axis=1)
    table[pl.ds(SLOT_ROW, 8)] = jnp.broadcast_to(slots, (8, W))


def kernel(lists, q, k, v, do, out_o, out_q, out_k, out_v, *scr):
    scr = list(scr)

    def take(n):
        got, scr[:] = scr[:n], scr[n:]
        return got

    landed = take(NIN)
    sent, got = take(NLIST), take(NLIST)
    give_v, give_k = take(2)
    back = take(NRET)
    sums = take(NRET)
    probs, pair, own_k, own_v, work, att, dq, table, tab, zs, zr, xs, xr, ls, ts = scr
    g, z = lax.axis_index("grp"), lax.axis_index("hd")
    mine = pl.ds(pl.multiple_of(z * W, W), W)
    ins = {"q": q, "k": k, "v": v, "do": do}
    outs = {"k": out_k, "v": out_v}
    gives = {"k": give_k, "v": give_v}
    inward = [(ins[a], r0, n, landed[i]) for i, (a, r0, n) in enumerate(INWARD)]
    outward = [(att, 0, ROWS, out_o), (dq, 0, ROWS, out_q)]
    outward += [(sums[i], r0, n, outs[a]) for i, (a, r0, n) in enumerate(RETURN)]
    across = [(sent[i], 0, INWARD[j][2], got[i]) for i, j in enumerate(LISTED)]
    across += [(gives[a], r0, n, back[i]) for i, (a, r0, n) in enumerate(RETURN)]
    job = {a: i for i, (a, _, _) in enumerate(INWARD)}

    def z_copy(j, i):
        t = (z + (Z_ORDER[i] if isinstance(i, int) else z_dist(i))) % HD
        if j < NIN:
            s, r0, n, to = inward[j]
            src, dst = s.at[pl.ds(r0, n), pl.ds(pl.multiple_of(t * W, W), W)], to.at[z]
        else:
            s, r0, n, to = outward[j - NIN]
            src, dst = s.at[t], to.at[z, pl.ds(r0, n)]
        return pltpu.make_async_remote_copy(
            src_ref=src, dst_ref=dst, send_sem=zs.at[j], recv_sem=zr.at[j],
            device_id={"grp": g, "hd": t}, device_id_type=MESH,
        )

    def own_copy(j):
        if j < NIN:
            s, r0, n, to = inward[j]
            return pltpu.make_async_copy(s.at[pl.ds(r0, n), mine], to.at[z], ls.at[j])
        s, r0, n, to = outward[j - NIN]
        return pltpu.make_async_copy(s.at[z], to.at[z, pl.ds(r0, n)], ls.at[j])

    def wait_bytes(ref, sem):
        pltpu.make_async_copy(ref, ref, sem).wait()

    def z_bytes(j):
        if j < NIN:
            return landed[j].at[pl.ds(0, 7)]
        return outward[j - NIN][0].at[pl.ds(0, 7)]

    def z_start(j):
        own_copy(j).start()
        for i in range(len(Z_ORDER)):
            z_copy(j, i).start()

    def z_arrive(j):
        own_copy(j).wait()
        wait_bytes(z_bytes(j), zr.at[j])

    def xy_copy(p, i):
        s, r0, n, to = across[p]
        r = XY_ORDER[i]
        return pltpu.make_async_remote_copy(
            src_ref=s.at[r, pl.ds(r0, n)], dst_ref=to.at[opposite(r)],
            send_sem=xs.at[p], recv_sem=xr.at[p],
            device_id={"grp": xy_group(g, r), "hd": z}, device_id_type=MESH,
        )

    def xy_bytes(p):
        return across[p][3].at[pl.ds(1, GRP - 1)]

    def xy_start(p):
        for i in range(len(XY_ORDER)):
            xy_copy(p, i).start()

    def xy_arrive(p):
        wait_bytes(xy_bytes(p), xr.at[p])

    greet(g, z)
    index_table(g, lists, table)
    to_tab = pltpu.make_async_copy(table, tab, ts.at[0])
    to_tab.start()
    met()
    for j in range(NIN):
        z_start(j)
    to_tab.wait()
    for p, j in enumerate(LISTED):
        z_arrive(j)
        for r in XY_ORDER:
            sent[p][r] = landed[j][tab[xy_group(g, r), PICKED] & (HD - 1)]
        xy_start(p)
        if j + 1 < NIN and INWARD[j + 1][0] == "q":
            z_arrive(j + 1)
    k_parts = [p for p, j in enumerate(LISTED) if INWARD[j][0] == "k"]
    v_parts = [p for p, j in enumerate(LISTED) if INWARD[j][0] == "v"]
    for p in k_parts:
        xy_arrive(p)
    qh, doh = landed[job["q"]], landed[job["do"]]

    def slots_of(b):
        return [None] + [tab[SLOT_ROW, b * NB + n] & (GRP - 1) for n in range(NB)]

    def rows_of(parts, b, slots, n):
        if n == 0:
            return jnp.concatenate([landed[LISTED[p]][b] for p in parts], axis=0)
        return jnp.concatenate([got[p][slots[n]] for p in parts], axis=0)

    def first_half(b, _):
        slots = slots_of(b)
        qb = qh[b]
        top = None
        for n in range(NB + 1):
            s = dot(rows_of(k_parts, b, slots, n), qb, 1, 1)
            work[n] = s
            m = jnp.max(s, axis=0, keepdims=True)
            top = m if top is None else jnp.maximum(top, m)
        shift = top * SCALE
        total = None
        for n in range(NB + 1):
            x = jnp.exp(work[n] * SCALE - shift)
            work[n] = x
            t = jnp.sum(x, axis=0, keepdims=True)
            total = t if total is None else total + t
        inv = 1.0 / total
        for n in range(NB + 1):
            probs[b, n] = (work[n] * inv).astype(BF16)
        return 0

    lax.fori_loop(0, HD, first_half, 0)
    z_arrive(job["do"])

    def collect(p, scale):
        to, r0, n, _ = across[p]
        rows = pl.ds(r0, n)

        def one(r, _):
            f = tab[r, FILL].astype(F32) * scale
            x = pair[tab[r, LISTER] & (PAIRS - 1), rows]
            for m in range(1, 4):
                x = x + pair[tab[r, LISTER + m] & (PAIRS - 1), rows]
            to[r, rows] = (x * f).astype(BF16)
            return 0

        lax.fori_loop(1, GRP, one, 0)

    for i, (a, r0, nr) in enumerate(RETURN):
        if a == "v":
            rows = pl.ds(r0, nr)

            def value_grads(b, _):
                dob = doh[b]
                for n in range(NB + 1):
                    x = dot(probs[b, n, rows], dob, 1, 0)
                    if n == 0:
                        own_v[b, rows] = x
                    else:
                        pair[b * NB + n - 1, rows] = x
                return 0

            lax.fori_loop(0, HD, value_grads, 0)
            collect(NLIST + i, 1.0)
            xy_start(NLIST + i)
    for p in v_parts:
        xy_arrive(p)

    def z_send(j, i):
        @pl.when(i < 7)
        def _():
            z_copy(j, i).start()

        @pl.when(i == 7)
        def _():
            own_copy(j).start()

    def second_half(i, _):
        b = (z + z_dist(i)) % HD
        slots = slots_of(b)
        qb, dob = qh[b], doh[b]
        out_t = None
        for n in range(NB + 1):
            o = dot(rows_of(v_parts, b, slots, n), probs[b, n], 0, 0)
            out_t = o if out_t is None else out_t + o
        delta = jnp.sum(out_t * dob.astype(F32).T, axis=0, keepdims=True)
        att[b] = out_t.T.astype(BF16)
        z_send(NIN, i)
        dq_t = None
        for n in range(NB + 1):
            dp = dot(rows_of(v_parts, b, slots, n), dob, 1, 1)
            ds = (probs[b, n].astype(F32) * (dp - delta)).astype(BF16)
            x = dot(rows_of(k_parts, b, slots, n), ds, 0, 0)
            dq_t = x if dq_t is None else dq_t + x
            x = dot(ds, qb, 1, 0)
            if n == 0:
                own_k[b] = x * SCALE
            else:
                pair[b * NB + n - 1] = x
        dq[b] = (dq_t * SCALE).T.astype(BF16)
        z_send(NIN + 1, i)
        return 0

    lax.fori_loop(0, HD, second_half, 0)
    for i, (a, r0, n) in enumerate(RETURN):
        if a == "k":
            collect(NLIST + i, SCALE)
            xy_start(NLIST + i)
    owns = {"k": own_k, "v": own_v}
    for i, (a, r0, n) in enumerate(RETURN):
        xy_arrive(NLIST + i)
        for r1 in range(0, n, 64):
            rows = pl.ds(r1, 64)

            def step(m, acc):
                acc = acc * tab[m, KEEP].astype(F32) + back[i][tab[m, ORDER] & (GRP - 1), rows].astype(F32)
                pair[m, rows] = acc
                return acc

            lax.fori_loop(0, GRP - 1, step, jnp.zeros((64, W), F32))
        for blk in range(HD):
            extra = pair[tab[blk, LAST] & (GRP - 1), pl.ds(0, n)] * tab[blk, HAS].astype(F32)
            sums[i][blk] = (owns[a][blk, pl.ds(r0, n)] + extra).astype(BF16)
        z_start(NIN + 2 + i)
    for j in range(NIN, NIN + len(outward)):
        z_arrive(j)
    for j in range(NIN + len(outward)):
        wait_bytes(z_bytes(j), zs.at[j])
    for p in range(len(across)):
        wait_bytes(xy_bytes(p), xs.at[p])


def run_kernel(lists, q, k, v, do):
    hbm = pl.BlockSpec(memory_space=pl.ANY)
    by_head = jax.ShapeDtypeStruct((HD, ROWS, W), BF16)
    dma = pltpu.SemaphoreType.DMA

    def tiles(n, rows=ROWS, dtype=BF16):
        return pltpu.VMEM((n, rows, W), dtype)

    nz, nx = NIN + 2 + NRET, NLIST + NRET
    return pl.pallas_call(
        kernel,
        name="graph_attention",
        out_shape=(by_head,) * 4,
        in_specs=[pl.BlockSpec(memory_space=pltpu.VMEM)] + [hbm] * 4,
        out_specs=(hbm,) * 4,
        scratch_shapes=[tiles(HD, n) for _, _, n in INWARD]
        + [tiles(GRP, INWARD[j][2]) for j in LISTED] * 2
        + [tiles(GRP), tiles(GRP)]
        + [tiles(GRP, n) for _, _, n in RETURN]
        + [tiles(HD, n) for _, _, n in RETURN]
        + [
            pltpu.VMEM((HD, NB + 1, ROWS, ROWS), BF16),
            tiles(PAIRS, ROWS, F32), tiles(HD, ROWS, F32), tiles(HD, ROWS, F32),
            pltpu.VMEM((NB + 1, ROWS, ROWS), F32),
            tiles(HD), tiles(HD),
            pltpu.VMEM((40, W), jnp.int32),
            pltpu.SMEM((40, W), jnp.int32),
            dma((nz,)), dma((nz,)), dma((nx,)), dma((nx,)), dma((nz,)), dma((1,)),
        ],
        compiler_params=pltpu.CompilerParams(collective_id=0, has_side_effects=True, vmem_limit_bytes=62 << 20),
    )(lists, q, k, v, do)


def lay_kernel(*refs):
    for src, dst in zip(refs[:4], refs[4:]):
        for h in range(HD):
            dst[:, h * W : (h + 1) * W] = src[h]


def lay(tiles):
    steps = 4
    rows = ROWS // steps
    return pl.pallas_call(
        lay_kernel,
        name="lay",
        grid=(steps,),
        out_shape=(jax.ShapeDtypeStruct((ROWS, HD * W), BF16),) * 4,
        in_specs=[pl.BlockSpec((HD, rows, W), lambda i: (0, i, 0))] * 4,
        out_specs=(pl.BlockSpec((rows, HD * W), lambda i: (i, 0)),) * 4,
        compiler_params=pltpu.CompilerParams(dimension_semantics=("arbitrary",), vmem_limit_bytes=62 << 20),
    )(*tiles)


def on_device(queries, keys, values, grad_out, neighbours):
    return tuple(lay(run_kernel(neighbours.T, queries, keys, values, grad_out)))


def solution(mesh):
    part = P(("grp", "hd"), None)
    return jax.shard_map(
        on_device, mesh=mesh, in_specs=(part,) * 4 + (P(),), out_specs=(part,) * 4, check_vma=False
    )
```

```python
import jax
import jax.numpy as jnp
from jax import lax
from jax.experimental import pallas as pl
from jax.experimental.pallas import tpu as pltpu
from jax.sharding import PartitionSpec as P

MESH = pl.DeviceIdType.MESH
HD = 8
GRP = 32
ROWS = 256
W = 128
F32 = jnp.float32
BF16 = jnp.bfloat16
SCALE = W ** (-0.5)

PLACES = [(0, 1), (1, 0), (0, 3), (3, 0), (0, 2), (2, 0), (1, 1), (3, 3), (1, 3), (3, 1), (2, 2), (1, 2), (2, 1), (3, 2), (2, 3), (0, 0)]
XY_ORDER = [dy * 8 + dx * 2 + dc for dc in (0, 1) for dy, dx in PLACES if dy + dx + dc > 0]
Z_ORDER = [1, 7, 2, 6, 3, 5, 4]


def z_dist(i):
    return jnp.where(i == 7, 0, jnp.where(i % 2 == 0, i // 2 + 1, 7 - i // 2))


def opposite(r):
    return ((4 - r // 8) % 4) * 8 + ((4 - (r // 2) % 4) % 4) * 2 + r % 2


def xy_group(g, r):
    c, x, y = g % 2, (g // 2) % 4, g // 8
    return (((y + r // 8) % 4) * 4 + (x + (r // 2) % 4) % 4) * 2 + (c + r % 2) % 2


def greet(g, z):
    barrier = pltpu.get_barrier_semaphore()
    for r in XY_ORDER:
        pl.semaphore_signal(barrier, inc=1, device_id={"grp": xy_group(g, r), "hd": z}, device_id_type=MESH)
    for d in Z_ORDER:
        pl.semaphore_signal(barrier, inc=1, device_id={"grp": g, "hd": (z + d) % HD}, device_id_type=MESH)


def met():
    pl.semaphore_wait(pltpu.get_barrier_semaphore(), len(XY_ORDER) + len(Z_ORDER))


NB = 8
PAIRS = HD * NB

INWARD = [("k", 0, 32), ("k", 32, 64), ("k", 96, 160), ("v", 0, 128), ("q", 0, 256), ("v", 128, 128), ("do", 0, 256)]
LISTED = [i for i, part in enumerate(INWARD) if part[0] in "kv"]
RETURN = [("v", 0, 128), ("v", 128, 128), ("k", 0, 128), ("k", 128, 64), ("k", 192, 64)]
NIN, NLIST, NRET = len(INWARD), len(LISTED), len(RETURN)

PICKED, LISTER, FILL, ORDER, KEEP, LAST, HAS = 0, 1, 5, 6, 7, 8, 9
SLOT_ROW = 32


def dot(a, b, ca, cb):
    return lax.dot_general(a, b, (((ca,), (cb,)), ((), ())), preferred_element_type=F32)


def index_table(g, lists, table):
    def iota(shape, dim):
        return lax.broadcasted_iota(jnp.int32, shape, dim)

    def down(x):
        return jnp.sum(x, axis=0, keepdims=True)

    def along(x):
        return jnp.sum(x, axis=1, keepdims=True)

    def most(x):
        return jnp.max(x, axis=1, keepdims=True)

    def ones(cond):
        return jnp.where(cond, 1, 0)

    def as_row(col):
        n = col.shape[0]
        return down(jnp.where(iota((n, n), 0) == iota((n, n), 1), col, 0))

    def place_of(blk):
        other = blk // HD
        dy = (other // 8 - g // 8 + 4) % 4
        dx = ((other // 2) % 4 - (g // 2) % 4 + 4) % 4
        return dy * 8 + dx * 2 + (other % 2 - g % 2 + 2) % 2

    nb = lists[...]
    best = jnp.max(jnp.where(nb // HD == g, nb % HD, -1), axis=0, keepdims=True)
    place = iota((GRP, 1), 0)
    by = iota((GRP, GRP * HD), 1) // HD
    picked = most(jnp.where(by == iota((GRP, GRP * HD), 0), best, -1))
    mine = most(jnp.where(by == xy_group(g, place), best, -1))
    lane = iota((NB, GRP * HD), 1)
    own = jnp.concatenate([along(jnp.where(lane == g * HD + b, nb, 0)) for b in range(HD)], axis=0)
    slot_col, slot_row = place_of(own), place_of(as_row(own))
    s64, l64 = iota((PAIRS, PAIRS), 0), iota((PAIRS, PAIRS), 1)
    rank = down(ones((slot_col == slot_row) & (s64 < l64)))
    mark = jnp.where(slot_row == iota((GRP, PAIRS), 0), rank, -1)
    lister = [most(jnp.where(mark == m, iota((GRP, PAIRS), 1), 0)) for m in range(4)]
    fill = most(ones(mark >= 0))
    s32, l32 = iota((GRP, GRP), 0), iota((GRP, GRP), 1)
    block = jnp.where(place == 0, HD + 1, jnp.where(mine < 0, HD, mine))
    block_row = as_row(block)
    key = block * GRP + place
    pos = down(ones(key < as_row(key)))
    at = pos == s32
    order = along(jnp.where(at, l32, 0))
    sorted_block = along(jnp.where(at, block_row, 0))
    keep = along(ones((pos + 1 == s32) & (block_row == sorted_block)))
    last = along(ones(block_row <= s32)) - 1
    has = most(ones(block_row == s32))
    cols = [jnp.maximum(picked, 0)] + lister + [fill, order, keep, jnp.maximum(last, 0), has]
    out = jnp.zeros((GRP, W), jnp.int32)
    for c, col in enumerate(cols):
        out = jnp.where(iota((GRP, W), 1) == c, col, out)
    table[pl.ds(0, GRP)] = out
    slots = jnp.concatenate([slot_row, jnp.zeros((1, W - PAIRS), jnp.int32)], axis=1)
    table[pl.ds(SLOT_ROW, 8)] = jnp.broadcast_to(slots, (8, W))


def kernel(lists, q, k, v, do, out_o, out_q, out_k, out_v, *scr):
    scr = list(scr)

    def take(n):
        got, scr[:] = scr[:n], scr[n:]
        return got

    landed = take(NIN)
    sent, got = take(NLIST), take(NLIST)
    give_v, give_k = take(2)
    back = take(NRET)
    sums = take(NRET)
    probs, pair, own_k, own_v, work, deltas, att, dq, table, tab, zs, zr, xs, xr, ls, ts = scr
    g, z = lax.axis_index("grp"), lax.axis_index("hd")
    mine = pl.ds(pl.multiple_of(z * W, W), W)
    ins = {"q": q, "k": k, "v": v, "do": do}
    outs = {"k": out_k, "v": out_v}
    gives = {"k": give_k, "v": give_v}
    inward = [(ins[a], r0, n, landed[i]) for i, (a, r0, n) in enumerate(INWARD)]
    outward = [(att, 0, ROWS, out_o), (dq, 0, ROWS, out_q)]
    outward += [(sums[i], r0, n, outs[a]) for i, (a, r0, n) in enumerate(RETURN)]
    across = [(sent[i], 0, INWARD[j][2], got[i]) for i, j in enumerate(LISTED)]
    across += [(gives[a], r0, n, back[i]) for i, (a, r0, n) in enumerate(RETURN)]
    job = {a: i for i, (a, _, _) in enumerate(INWARD)}

    def z_copy(j, i):
        t = (z + (Z_ORDER[i] if isinstance(i, int) else z_dist(i))) % HD
        if j < NIN:
            s, r0, n, to = inward[j]
            src, dst = s.at[pl.ds(r0, n), pl.ds(pl.multiple_of(t * W, W), W)], to.at[z]
        else:
            s, r0, n, to = outward[j - NIN]
            src, dst = s.at[t], to.at[z, pl.ds(r0, n)]
        return pltpu.make_async_remote_copy(
            src_ref=src, dst_ref=dst, send_sem=zs.at[j], recv_sem=zr.at[j],
            device_id={"grp": g, "hd": t}, device_id_type=MESH,
        )

    def own_copy(j):
        if j < NIN:
            s, r0, n, to = inward[j]
            return pltpu.make_async_copy(s.at[pl.ds(r0, n), mine], to.at[z], ls.at[j])
        s, r0, n, to = outward[j - NIN]
        return pltpu.make_async_copy(s.at[z], to.at[z, pl.ds(r0, n)], ls.at[j])

    def wait_bytes(ref, sem):
        pltpu.make_async_copy(ref, ref, sem).wait()

    def z_bytes(j):
        if j < NIN:
            return landed[j].at[pl.ds(0, 7)]
        return outward[j - NIN][0].at[pl.ds(0, 7)]

    def z_start(j):
        own_copy(j).start()
        for i in range(len(Z_ORDER)):
            z_copy(j, i).start()

    def z_arrive(j):
        own_copy(j).wait()
        wait_bytes(z_bytes(j), zr.at[j])

    def xy_copy(p, i):
        s, r0, n, to = across[p]
        r = XY_ORDER[i]
        return pltpu.make_async_remote_copy(
            src_ref=s.at[r, pl.ds(r0, n)], dst_ref=to.at[opposite(r)],
            send_sem=xs.at[p], recv_sem=xr.at[p],
            device_id={"grp": xy_group(g, r), "hd": z}, device_id_type=MESH,
        )

    def xy_bytes(p):
        return across[p][3].at[pl.ds(1, GRP - 1)]

    def xy_start(p):
        for i in range(len(XY_ORDER)):
            xy_copy(p, i).start()

    def xy_arrive(p):
        wait_bytes(xy_bytes(p), xr.at[p])

    greet(g, z)
    index_table(g, lists, table)
    to_tab = pltpu.make_async_copy(table, tab, ts.at[0])
    to_tab.start()
    met()
    for j in range(3):
        z_start(j)
    to_tab.wait()
    for p, j in enumerate(LISTED):
        z_arrive(j)
        for r in XY_ORDER:
            sent[p][r] = landed[j][tab[xy_group(g, r), PICKED] & (HD - 1)]
        xy_start(p)
        if p == 0:
            for later in range(3, NIN):
                z_start(later)
        if j + 1 < NIN and INWARD[j + 1][0] == "q":
            z_arrive(j + 1)
    k_parts = [p for p, j in enumerate(LISTED) if INWARD[j][0] == "k"]
    v_parts = [p for p, j in enumerate(LISTED) if INWARD[j][0] == "v"]
    for p in k_parts:
        xy_arrive(p)
    qh, doh = landed[job["q"]], landed[job["do"]]

    def slots_of(b):
        return [None] + [tab[SLOT_ROW, b * NB + n] & (GRP - 1) for n in range(NB)]

    def rows_of(parts, b, slots, n):
        if n == 0:
            return jnp.concatenate([landed[LISTED[p]][b] for p in parts], axis=0)
        return jnp.concatenate([got[p][slots[n]] for p in parts], axis=0)

    def first_half(b, _):
        slots = slots_of(b)
        qb = qh[b]
        top = None
        for n in range(NB + 1):
            s = dot(rows_of(k_parts, b, slots, n), qb, 1, 1)
            work[n] = s
            m = jnp.max(s, axis=0, keepdims=True)
            top = m if top is None else jnp.maximum(top, m)
        shift = top * SCALE
        total = None
        for n in range(NB + 1):
            x = jnp.exp(work[n] * SCALE - shift)
            work[n] = x
            t = jnp.sum(x, axis=0, keepdims=True)
            total = t if total is None else total + t
        inv = 1.0 / total
        for n in range(NB + 1):
            probs[b, n] = (work[n] * inv).astype(BF16)
        return 0

    lax.fori_loop(0, HD, first_half, 0)
    z_arrive(job["do"])

    def collect(p, scale):
        to, r0, n, _ = across[p]
        rows = pl.ds(r0, n)

        def one(r, _):
            f = tab[r, FILL].astype(F32) * scale
            x = pair[tab[r, LISTER] & (PAIRS - 1), rows]
            for m in range(1, 4):
                x = x + pair[tab[r, LISTER + m] & (PAIRS - 1), rows]
            to[r, rows] = (x * f).astype(BF16)
            return 0

        lax.fori_loop(1, GRP, one, 0)

    for i, (a, r0, nr) in enumerate(RETURN):
        if a == "v":
            rows = pl.ds(r0, nr)

            def value_grads(b, _):
                dob = doh[b]
                for n in range(NB + 1):
                    x = dot(probs[b, n, rows], dob, 1, 0)
                    if n == 0:
                        own_v[b, rows] = x
                    else:
                        pair[b * NB + n - 1, rows] = x
                return 0

            lax.fori_loop(0, HD, value_grads, 0, unroll=2)
            collect(NLIST + i, 1.0)
            xy_start(NLIST + i)
    for p in v_parts:
        xy_arrive(p)

    def z_send(j, i):
        @pl.when(i < 7)
        def _():
            z_copy(j, i).start()

        @pl.when(i == 7)
        def _():
            own_copy(j).start()

    def outputs(i, _):
        b = (z + z_dist(i)) % HD
        slots = slots_of(b)
        dob = doh[b]
        out_t = None
        for n in range(NB + 1):
            o = dot(rows_of(v_parts, b, slots, n), probs[b, n], 0, 0)
            out_t = o if out_t is None else out_t + o
        delta = jnp.sum(out_t * dob.astype(F32).T, axis=0, keepdims=True)
        att[b] = out_t.T.astype(BF16)
        deltas[b] = delta
        z_send(NIN, i)
        return 0

    lax.fori_loop(0, HD, outputs, 0, unroll=2)

    def second_half(i, _):
        b = (z + z_dist(i)) % HD
        slots = slots_of(b)
        qb, dob, delta = qh[b], doh[b], deltas[b]
        dq_t = None
        for n in range(NB + 1):
            dp = dot(rows_of(v_parts, b, slots, n), dob, 1, 1)
            ds = (probs[b, n].astype(F32) * (dp - delta)).astype(BF16)
            x = dot(rows_of(k_parts, b, slots, n), ds, 0, 0)
            dq_t = x if dq_t is None else dq_t + x
            x = dot(ds, qb, 1, 0)
            if n == 0:
                own_k[b] = x * SCALE
            else:
                pair[b * NB + n - 1] = x
        dq[b] = (dq_t * SCALE).T.astype(BF16)
        z_send(NIN + 1, i)
        return 0

    lax.fori_loop(0, HD, second_half, 0, unroll=2)
    for i, (a, r0, n) in enumerate(RETURN):
        if a == "k":
            collect(NLIST + i, SCALE)
            xy_start(NLIST + i)
    owns = {"k": own_k, "v": own_v}
    for i, (a, r0, n) in enumerate(RETURN):
        xy_arrive(NLIST + i)
        for r1 in range(0, n, 64):
            rows = pl.ds(r1, 64)

            def step(m, acc):
                acc = acc * tab[m, KEEP].astype(F32) + back[i][tab[m, ORDER] & (GRP - 1), rows].astype(F32)
                pair[m, rows] = acc
                return acc

            lax.fori_loop(0, GRP - 1, step, jnp.zeros((64, W), F32))
        for blk in range(HD):
            extra = pair[tab[blk, LAST] & (GRP - 1), pl.ds(0, n)] * tab[blk, HAS].astype(F32)
            sums[i][blk] = (owns[a][blk, pl.ds(r0, n)] + extra).astype(BF16)
        z_start(NIN + 2 + i)
    for j in range(NIN, NIN + len(outward)):
        z_arrive(j)
    for j in range(NIN + len(outward)):
        wait_bytes(z_bytes(j), zs.at[j])
    for p in range(len(across)):
        wait_bytes(xy_bytes(p), xs.at[p])


def run_kernel(lists, q, k, v, do):
    hbm = pl.BlockSpec(memory_space=pl.ANY)
    by_head = jax.ShapeDtypeStruct((HD, ROWS, W), BF16)
    dma = pltpu.SemaphoreType.DMA

    def tiles(n, rows=ROWS, dtype=BF16):
        return pltpu.VMEM((n, rows, W), dtype)

    nz, nx = NIN + 2 + NRET, NLIST + NRET
    return pl.pallas_call(
        kernel,
        name="graph_attention",
        out_shape=(by_head,) * 4,
        in_specs=[pl.BlockSpec(memory_space=pltpu.VMEM)] + [hbm] * 4,
        out_specs=(hbm,) * 4,
        scratch_shapes=[tiles(HD, n) for _, _, n in INWARD]
        + [tiles(GRP, INWARD[j][2]) for j in LISTED] * 2
        + [tiles(GRP), tiles(GRP)]
        + [tiles(GRP, n) for _, _, n in RETURN]
        + [tiles(HD, n) for _, _, n in RETURN]
        + [
            pltpu.VMEM((HD, NB + 1, ROWS, ROWS), BF16),
            tiles(PAIRS, ROWS, F32), tiles(HD, ROWS, F32), tiles(HD, ROWS, F32),
            pltpu.VMEM((NB + 1, ROWS, ROWS), F32),
            pltpu.VMEM((HD, 1, ROWS), F32),
            tiles(HD), tiles(HD),
            pltpu.VMEM((40, W), jnp.int32),
            pltpu.SMEM((40, W), jnp.int32),
            dma((nz,)), dma((nz,)), dma((nx,)), dma((nx,)), dma((nz,)), dma((1,)),
        ],
        compiler_params=pltpu.CompilerParams(collective_id=0, has_side_effects=True, vmem_limit_bytes=62 << 20),
    )(lists, q, k, v, do)


def lay_kernel(*refs):
    for src, dst in zip(refs[:4], refs[4:]):
        for h in range(HD):
            dst[:, h * W : (h + 1) * W] = src[h]


def lay(tiles):
    steps = 2
    rows = ROWS // steps
    return pl.pallas_call(
        lay_kernel,
        name="lay",
        grid=(steps,),
        out_shape=(jax.ShapeDtypeStruct((ROWS, HD * W), BF16),) * 4,
        in_specs=[pl.BlockSpec((HD, rows, W), lambda i: (0, i, 0))] * 4,
        out_specs=(pl.BlockSpec((rows, HD * W), lambda i: (i, 0)),) * 4,
        compiler_params=pltpu.CompilerParams(dimension_semantics=("arbitrary",), vmem_limit_bytes=62 << 20),
    )(*tiles)


def on_device(queries, keys, values, grad_out, neighbours):
    return tuple(lay(run_kernel(neighbours.T, queries, keys, values, grad_out)))


def solution(mesh):
    part = P(("grp", "hd"), None)
    return jax.shard_map(
        on_device, mesh=mesh, in_specs=(part,) * 4 + (P(),), out_specs=(part,) * 4, check_vma=False
    )
```

```python
import jax
import jax.numpy as jnp
from jax import lax
from jax.experimental import pallas as pl
from jax.experimental.pallas import tpu as pltpu
from jax.sharding import PartitionSpec as P

MESH = pl.DeviceIdType.MESH
HD = 8
GRP = 32
ROWS = 256
W = 128
F32 = jnp.float32
BF16 = jnp.bfloat16
SCALE = W ** (-0.5)

PLACES = [(0, 1), (1, 0), (0, 3), (3, 0), (0, 2), (2, 0), (1, 1), (3, 3), (1, 3), (3, 1), (2, 2), (1, 2), (2, 1), (3, 2), (2, 3), (0, 0)]
XY_ORDER = [dy * 8 + dx * 2 + dc for dc in (0, 1) for dy, dx in PLACES if dy + dx + dc > 0]
Z_ORDER = [1, 7, 2, 6, 3, 5, 4]


def z_dist(i):
    return jnp.where(i == 7, 0, jnp.where(i % 2 == 0, i // 2 + 1, 7 - i // 2))


def opposite(r):
    return ((4 - r // 8) % 4) * 8 + ((4 - (r // 2) % 4) % 4) * 2 + r % 2


def xy_group(g, r):
    c, x, y = g % 2, (g // 2) % 4, g // 8
    return (((y + r // 8) % 4) * 4 + (x + (r // 2) % 4) % 4) * 2 + (c + r % 2) % 2


def greet(g, z):
    barrier = pltpu.get_barrier_semaphore()
    for r in XY_ORDER:
        pl.semaphore_signal(barrier, inc=1, device_id={"grp": xy_group(g, r), "hd": z}, device_id_type=MESH)
    for d in Z_ORDER:
        pl.semaphore_signal(barrier, inc=1, device_id={"grp": g, "hd": (z + d) % HD}, device_id_type=MESH)


def met():
    pl.semaphore_wait(pltpu.get_barrier_semaphore(), len(XY_ORDER) + len(Z_ORDER))


NB = 8
PAIRS = HD * NB

INWARD = [("k", 0, 32), ("k", 32, 64), ("k", 96, 160), ("v", 0, 128), ("q", 0, 256), ("v", 128, 128), ("do", 0, 256)]
LISTED = [i for i, part in enumerate(INWARD) if part[0] in "kv"]
RETURN = [("v", 0, 128), ("v", 128, 128), ("k", 0, 128), ("k", 128, 64), ("k", 192, 64)]
NIN, NLIST, NRET = len(INWARD), len(LISTED), len(RETURN)

PICKED, LISTER, FILL, ORDER, KEEP, LAST, HAS = 0, 1, 5, 6, 7, 8, 9
SLOT_ROW = 32


def dot(a, b, ca, cb):
    return lax.dot_general(a, b, (((ca,), (cb,)), ((), ())), preferred_element_type=F32)


def index_table(g, lists, table):
    def iota(shape, dim):
        return lax.broadcasted_iota(jnp.int32, shape, dim)

    def down(x):
        return jnp.sum(x, axis=0, keepdims=True)

    def along(x):
        return jnp.sum(x, axis=1, keepdims=True)

    def most(x):
        return jnp.max(x, axis=1, keepdims=True)

    def ones(cond):
        return jnp.where(cond, 1, 0)

    def as_row(col):
        n = col.shape[0]
        return down(jnp.where(iota((n, n), 0) == iota((n, n), 1), col, 0))

    def place_of(blk):
        other = blk // HD
        dy = (other // 8 - g // 8 + 4) % 4
        dx = ((other // 2) % 4 - (g // 2) % 4 + 4) % 4
        return dy * 8 + dx * 2 + (other % 2 - g % 2 + 2) % 2

    nb = lists[...]
    best = jnp.max(jnp.where(nb // HD == g, nb % HD, -1), axis=0, keepdims=True)
    place = iota((GRP, 1), 0)
    by = iota((GRP, GRP * HD), 1) // HD
    picked = most(jnp.where(by == iota((GRP, GRP * HD), 0), best, -1))
    mine = most(jnp.where(by == xy_group(g, place), best, -1))
    lane = iota((NB, GRP * HD), 1)
    own = jnp.concatenate([along(jnp.where(lane == g * HD + b, nb, 0)) for b in range(HD)], axis=0)
    slot_col, slot_row = place_of(own), place_of(as_row(own))
    s64, l64 = iota((PAIRS, PAIRS), 0), iota((PAIRS, PAIRS), 1)
    rank = down(ones((slot_col == slot_row) & (s64 < l64)))
    mark = jnp.where(slot_row == iota((GRP, PAIRS), 0), rank, -1)
    lister = [most(jnp.where(mark == m, iota((GRP, PAIRS), 1), 0)) for m in range(4)]
    fill = most(ones(mark >= 0))
    s32, l32 = iota((GRP, GRP), 0), iota((GRP, GRP), 1)
    block = jnp.where(place == 0, HD + 1, jnp.where(mine < 0, HD, mine))
    block_row = as_row(block)
    key = block * GRP + place
    pos = down(ones(key < as_row(key)))
    at = pos == s32
    order = along(jnp.where(at, l32, 0))
    sorted_block = along(jnp.where(at, block_row, 0))
    keep = along(ones((pos + 1 == s32) & (block_row == sorted_block)))
    last = along(ones(block_row <= s32)) - 1
    has = most(ones(block_row == s32))
    cols = [jnp.maximum(picked, 0)] + lister + [fill, order, keep, jnp.maximum(last, 0), has]
    out = jnp.zeros((GRP, W), jnp.int32)
    for c, col in enumerate(cols):
        out = jnp.where(iota((GRP, W), 1) == c, col, out)
    table[pl.ds(0, GRP)] = out
    slots = jnp.concatenate([slot_row, jnp.zeros((1, W - PAIRS), jnp.int32)], axis=1)
    table[pl.ds(SLOT_ROW, 8)] = jnp.broadcast_to(slots, (8, W))


def kernel(lists, q, k, v, do, out_o, out_q, out_k, out_v, *scr):
    scr = list(scr)

    def take(n):
        got, scr[:] = scr[:n], scr[n:]
        return got

    landed = take(NIN)
    sent, got = take(NLIST), take(NLIST)
    give_v, give_k = take(2)
    back = take(NRET)
    sums = take(NRET)
    probs, pair, own_k, own_v, work, deltas, att, dq, table, tab, zs, zr, xs, xr, ls, ts = scr
    g, z = lax.axis_index("grp"), lax.axis_index("hd")
    mine = pl.ds(pl.multiple_of(z * W, W), W)
    ins = {"q": q, "k": k, "v": v, "do": do}
    outs = {"k": out_k, "v": out_v}
    gives = {"k": give_k, "v": give_v}
    inward = [(ins[a], r0, n, landed[i]) for i, (a, r0, n) in enumerate(INWARD)]
    outward = [(att, 0, ROWS, out_o), (dq, 0, ROWS, out_q)]
    outward += [(sums[i], r0, n, outs[a]) for i, (a, r0, n) in enumerate(RETURN)]
    across = [(sent[i], 0, INWARD[j][2], got[i]) for i, j in enumerate(LISTED)]
    across += [(gives[a], r0, n, back[i]) for i, (a, r0, n) in enumerate(RETURN)]
    job = {a: i for i, (a, _, _) in enumerate(INWARD)}

    def z_copy(j, i):
        t = (z + (Z_ORDER[i] if isinstance(i, int) else z_dist(i))) % HD
        if j < NIN:
            s, r0, n, to = inward[j]
            src, dst = s.at[pl.ds(r0, n), pl.ds(pl.multiple_of(t * W, W), W)], to.at[z]
        else:
            s, r0, n, to = outward[j - NIN]
            src, dst = s.at[t], to.at[z, pl.ds(r0, n)]
        return pltpu.make_async_remote_copy(
            src_ref=src, dst_ref=dst, send_sem=zs.at[j], recv_sem=zr.at[j],
            device_id={"grp": g, "hd": t}, device_id_type=MESH,
        )

    def own_copy(j):
        if j < NIN:
            s, r0, n, to = inward[j]
            return pltpu.make_async_copy(s.at[pl.ds(r0, n), mine], to.at[z], ls.at[j])
        s, r0, n, to = outward[j - NIN]
        return pltpu.make_async_copy(s.at[z], to.at[z, pl.ds(r0, n)], ls.at[j])

    def wait_bytes(ref, sem):
        pltpu.make_async_copy(ref, ref, sem).wait()

    def z_bytes(j):
        if j < NIN:
            return landed[j].at[pl.ds(0, 7)]
        return outward[j - NIN][0].at[pl.ds(0, 7)]

    def z_start(j):
        own_copy(j).start()
        for i in range(len(Z_ORDER))[::-1]:
            z_copy(j, i).start()

    def z_arrive(j):
        own_copy(j).wait()
        wait_bytes(z_bytes(j), zr.at[j])

    def xy_copy(p, i):
        s, r0, n, to = across[p]
        r = XY_ORDER[i]
        return pltpu.make_async_remote_copy(
            src_ref=s.at[r, pl.ds(r0, n)], dst_ref=to.at[opposite(r)],
            send_sem=xs.at[p], recv_sem=xr.at[p],
            device_id={"grp": xy_group(g, r), "hd": z}, device_id_type=MESH,
        )

    def xy_bytes(p):
        return across[p][3].at[pl.ds(1, GRP - 1)]

    def xy_start(p):
        for i in range(len(XY_ORDER))[::-1]:
            xy_copy(p, i).start()

    def xy_arrive(p):
        wait_bytes(xy_bytes(p), xr.at[p])

    greet(g, z)
    index_table(g, lists, table)
    to_tab = pltpu.make_async_copy(table, tab, ts.at[0])
    to_tab.start()
    met()
    for j in range(3):
        z_start(j)
    to_tab.wait()
    for p, j in enumerate(LISTED):
        z_arrive(j)
        for r in XY_ORDER:
            sent[p][r] = landed[j][tab[xy_group(g, r), PICKED] & (HD - 1)]
        xy_start(p)
        if p == 0:
            for later in range(3, NIN):
                z_start(later)
        if j + 1 < NIN and INWARD[j + 1][0] == "q":
            z_arrive(j + 1)
    k_parts = [p for p, j in enumerate(LISTED) if INWARD[j][0] == "k"]
    v_parts = [p for p, j in enumerate(LISTED) if INWARD[j][0] == "v"]
    for p in k_parts:
        xy_arrive(p)
    qh, doh = landed[job["q"]], landed[job["do"]]

    def slots_of(b):
        return [None] + [tab[SLOT_ROW, b * NB + n] & (GRP - 1) for n in range(NB)]

    def rows_of(parts, b, slots, n):
        if n == 0:
            return jnp.concatenate([landed[LISTED[p]][b] for p in parts], axis=0)
        return jnp.concatenate([got[p][slots[n]] for p in parts], axis=0)

    def first_half(b, _):
        slots = slots_of(b)
        qb = qh[b]
        top = None
        for n in range(NB + 1):
            s = dot(rows_of(k_parts, b, slots, n), qb, 1, 1)
            work[n] = s
            m = jnp.max(s, axis=0, keepdims=True)
            top = m if top is None else jnp.maximum(top, m)
        shift = top * SCALE
        total = None
        for n in range(NB + 1):
            x = jnp.exp(work[n] * SCALE - shift)
            work[n] = x
            t = jnp.sum(x, axis=0, keepdims=True)
            total = t if total is None else total + t
        inv = 1.0 / total
        for n in range(NB + 1):
            probs[b, n] = (work[n] * inv).astype(BF16)
        return 0

    lax.fori_loop(0, HD, first_half, 0)
    z_arrive(job["do"])

    def collect(p, scale):
        to, r0, n, _ = across[p]
        rows = pl.ds(r0, n)

        def one(r, _):
            f = tab[r, FILL].astype(F32) * scale
            x = pair[tab[r, LISTER] & (PAIRS - 1), rows]
            for m in range(1, 4):
                x = x + pair[tab[r, LISTER + m] & (PAIRS - 1), rows]
            to[r, rows] = (x * f).astype(BF16)
            return 0

        lax.fori_loop(1, GRP, one, 0, unroll=4)

    for i, (a, r0, nr) in enumerate(RETURN):
        if a == "v":
            rows = pl.ds(r0, nr)

            def value_grads(b, _):
                dob = doh[b]
                for n in range(NB + 1):
                    x = dot(probs[b, n, rows], dob, 1, 0)
                    if n == 0:
                        own_v[b, rows] = x
                    else:
                        pair[b * NB + n - 1, rows] = x
                return 0

            lax.fori_loop(0, HD, value_grads, 0, unroll=2)
            collect(NLIST + i, 1.0)
            xy_start(NLIST + i)
    for p in v_parts:
        xy_arrive(p)

    def z_send(j, i):
        @pl.when(i < 7)
        def _():
            z_copy(j, i).start()

        @pl.when(i == 7)
        def _():
            own_copy(j).start()

    def outputs(i, _):
        b = (z + z_dist(i)) % HD
        slots = slots_of(b)
        dob = doh[b]
        out_t = None
        for n in range(NB + 1):
            o = dot(rows_of(v_parts, b, slots, n), probs[b, n], 0, 0)
            out_t = o if out_t is None else out_t + o
        delta = jnp.sum(out_t * dob.astype(F32).T, axis=0, keepdims=True)
        att[b] = out_t.T.astype(BF16)
        deltas[b] = delta
        z_send(NIN, i)
        return 0

    lax.fori_loop(0, HD, outputs, 0, unroll=2)

    def second_half(i, _):
        b = (z + z_dist(i)) % HD
        slots = slots_of(b)
        qb, dob, delta = qh[b], doh[b], deltas[b]
        dq_t = None
        for n in range(NB + 1):
            dp = dot(rows_of(v_parts, b, slots, n), dob, 1, 1)
            ds = (probs[b, n].astype(F32) * (dp - delta)).astype(BF16)
            x = dot(rows_of(k_parts, b, slots, n), ds, 0, 0)
            dq_t = x if dq_t is None else dq_t + x
            x = dot(ds, qb, 1, 0)
            if n == 0:
                own_k[b] = x * SCALE
            else:
                pair[b * NB + n - 1] = x
        dq[b] = (dq_t * SCALE).T.astype(BF16)
        z_send(NIN + 1, i)
        return 0

    lax.fori_loop(0, HD, second_half, 0, unroll=2)
    for i, (a, r0, n) in enumerate(RETURN):
        if a == "k":
            collect(NLIST + i, SCALE)
            xy_start(NLIST + i)
    owns = {"k": own_k, "v": own_v}
    for i, (a, r0, n) in enumerate(RETURN):
        xy_arrive(NLIST + i)
        for r1 in range(0, n, 64):
            rows = pl.ds(r1, 64)

            def step(m, acc):
                acc = acc * tab[m, KEEP].astype(F32) + back[i][tab[m, ORDER] & (GRP - 1), rows].astype(F32)
                pair[m, rows] = acc
                return acc

            lax.fori_loop(0, GRP - 1, step, jnp.zeros((64, W), F32), unroll=True)
        for blk in range(HD):
            extra = pair[tab[blk, LAST] & (GRP - 1), pl.ds(0, n)] * tab[blk, HAS].astype(F32)
            sums[i][blk] = (owns[a][blk, pl.ds(r0, n)] + extra).astype(BF16)
        z_start(NIN + 2 + i)
    for j in range(NIN, NIN + len(outward)):
        z_arrive(j)
    for j in range(NIN + len(outward)):
        wait_bytes(z_bytes(j), zs.at[j])
    for p in range(len(across)):
        wait_bytes(xy_bytes(p), xs.at[p])


def run_kernel(lists, q, k, v, do):
    hbm = pl.BlockSpec(memory_space=pl.ANY)
    by_head = jax.ShapeDtypeStruct((HD, ROWS, W), BF16)
    dma = pltpu.SemaphoreType.DMA

    def tiles(n, rows=ROWS, dtype=BF16):
        return pltpu.VMEM((n, rows, W), dtype)

    nz, nx = NIN + 2 + NRET, NLIST + NRET
    return pl.pallas_call(
        kernel,
        name="graph_attention",
        out_shape=(by_head,) * 4,
        in_specs=[pl.BlockSpec(memory_space=pltpu.VMEM)] + [hbm] * 4,
        out_specs=(hbm,) * 4,
        scratch_shapes=[tiles(HD, n) for _, _, n in INWARD]
        + [tiles(GRP, INWARD[j][2]) for j in LISTED] * 2
        + [tiles(GRP), tiles(GRP)]
        + [tiles(GRP, n) for _, _, n in RETURN]
        + [tiles(HD, n) for _, _, n in RETURN]
        + [
            pltpu.VMEM((HD, NB + 1, ROWS, ROWS), BF16),
            tiles(PAIRS, ROWS, F32), tiles(HD, ROWS, F32), tiles(HD, ROWS, F32),
            pltpu.VMEM((NB + 1, ROWS, ROWS), F32),
            pltpu.VMEM((HD, 1, ROWS), F32),
            tiles(HD), tiles(HD),
            pltpu.VMEM((40, W), jnp.int32),
            pltpu.SMEM((40, W), jnp.int32),
            dma((nz,)), dma((nz,)), dma((nx,)), dma((nx,)), dma((nz,)), dma((1,)),
        ],
        compiler_params=pltpu.CompilerParams(collective_id=0, has_side_effects=True, vmem_limit_bytes=62 << 20),
    )(lists, q, k, v, do)


def lay_kernel(*refs):
    for src, dst in zip(refs[:4], refs[4:]):
        for h in range(HD):
            dst[:, h * W : (h + 1) * W] = src[h]


def lay(tiles):
    steps = 2
    rows = ROWS // steps
    return pl.pallas_call(
        lay_kernel,
        name="lay",
        grid=(steps,),
        out_shape=(jax.ShapeDtypeStruct((ROWS, HD * W), BF16),) * 4,
        in_specs=[pl.BlockSpec((HD, rows, W), lambda i: (0, i, 0))] * 4,
        out_specs=(pl.BlockSpec((rows, HD * W), lambda i: (i, 0)),) * 4,
        compiler_params=pltpu.CompilerParams(dimension_semantics=("arbitrary",), vmem_limit_bytes=62 << 20),
    )(*tiles)


def on_device(queries, keys, values, grad_out, neighbours):
    return tuple(lay(run_kernel(neighbours.T, queries, keys, values, grad_out)))


def solution(mesh):
    part = P(("grp", "hd"), None)
    return jax.shard_map(
        on_device, mesh=mesh, in_specs=(part,) * 4 + (P(),), out_specs=(part,) * 4, check_vma=False
    )
```
